32 devices in a mesh: blk: 8 (over z, y), exp: 4 (over x, core).
Axes of the slice: x: 2, y: 2, z: 4, core: 2. Of those that a mesh axis runs over, the one named last changes fastest.
Arguments:
- grad_block: bfloat16 [128, 256, 2048], P('exp', 'blk'), may hold values from -6 to 6
- momentum: float32 [128, 256, 2048], P('exp', 'blk'), may hold values from -6 to 6
- model_root: bfloat16 [2048, 2048], P('blk'), may hold values from -0.125 to 0.125
- expert_root: bfloat16 [128, 128], replicated, may hold values from -0.5 to 0.5
Outputs:
- momentum_new: float32 [128, 256, 2048], P('exp', 'blk')
The draws below stay inside these ranges and needn't reach their ends.
All inputs are finite; a program needn't handle non-finite values.
Results may differ from the reference program's by a relative error of at most 0.0031.
Values may be sent and summed in bfloat16 or wider, within the bound.
A program may use at most 128 MiB of HBM per device.

```python
import jax
import jax.numpy as jnp

D = 2048
HW = 256
EXPERTS = 128


def levels(rng, dims, cuts, low, largest):
    level, own = 1.0, jax.random.fold_in(rng, 6)
    for dim, shards_of in cuts:
        steps = jnp.exp(jax.random.uniform(jax.random.fold_in(own, dim), (shards_of,), jnp.float32, low / len(cuts), largest / len(cuts)))
        level = level * jnp.repeat(steps, dims[dim] // shards_of).reshape([-1 if axis == dim else 1 for axis in range(len(dims))])
    return level


def bell_draw(stream_key, shape, deviation, most, split=(), held_as=jnp.bfloat16):
    values = deviation * jax.random.normal(stream_key, shape, jnp.float32)
    if split:
        values = values * levels(stream_key, shape, split, -0.22, 0.18)
    return jnp.clip(values, -most, most).astype(held_as)


def setup_inputs(seed: int = 0) -> dict:
    streams_of = jax.random.split(jax.random.key(seed), 5)
    grad_block = bell_draw(streams_of[0], (EXPERTS, HW, D), 1.0, 6.0, ((0, 4), (1, 8)))
    momentum = bell_draw(streams_of[1], (EXPERTS, HW, D), 1.0, 6.0, ((0, 4), (1, 8)), jnp.float32)
    model_root = bell_draw(streams_of[2], (D, D), D ** -0.5, 0.125, ((0, 8),))
    expert_root = bell_draw(streams_of[3], (EXPERTS, EXPERTS), EXPERTS ** -0.5, 0.5)
    return dict(grad_block=grad_block, momentum=momentum, model_root=model_root, expert_root=expert_root)


def reference(grad_block, momentum, model_root, expert_root):
    experts, hidden, width = grad_block.shape
    flat_rows = grad_block.reshape(experts * hidden, width)
    model_mode = jnp.dot(flat_rows, model_root.T, preferred_element_type=jnp.float32).astype(jnp.bfloat16)
    stacked = model_mode.reshape(experts, hidden * width)
    expert_mode = jnp.dot(expert_root, stacked, preferred_element_type=jnp.float32).astype(jnp.bfloat16)
    expert_mode = expert_mode.reshape(experts, hidden, width)
    return 0.9 * momentum + expert_mode.astype(jnp.float32)
```

```python
import functools

import jax
import jax.numpy as jnp
from jax import lax
from jax.experimental import pallas as pl
from jax.experimental.pallas import tpu as pltpu
from jax.sharding import PartitionSpec as P

MESH = pl.DeviceIdType.MESH
SUB = 16
TILE = 256


def kernel(
    n_blk, n_exp, n_chunks,
    grad, momentum, root_rows, expert_hbm, out,
    expert_root, gathered, root, mix, blended,
    x_send, x_recv, p_send, p_recv, f_send, f_recv, own_sem,
    z_send, z_recv, y_send, y_recv, c_send, c_recv, root_sem, mom_sem, mix_sem,
):
    local_experts, local_hidden, width = grad.shape
    groups = local_hidden // SUB
    chunk = width // n_chunks
    chips = n_exp // 2
    n_z = n_blk // 2
    rows = local_experts * SUB
    half = root.shape[2]
    batch = 4 if n_exp % 4 == 0 else 2
    depth = batch * rows
    slice_rows = 2 * half

    me = lax.axis_index("exp")
    chip, core = me // 2, me % 2
    blk = lax.axis_index("blk")
    zi, yi = blk // 2, blk % 2
    mate = {"exp": chip * 2 + 1 - core}
    y_peer = {"blk": zi * 2 + 1 - yi}

    def chip_at(offset):
        return lax.rem(chip + offset + chips, chips)

    def z_at(offset):
        return lax.rem(zi + offset + n_z, n_z)

    def remote(src, dst, send, recv, device):
        return pltpu.make_async_remote_copy(
            src_ref=src, dst_ref=dst, send_sem=send, recv_sem=recv, device_id=device, device_id_type=MESH
        )

    barrier = pltpu.get_barrier_semaphore()
    peers = [mate, y_peer]
    peers += [{"exp": chip_at(c) * 2 + core} for c in range(1, chips)]
    peers += [{"blk": z_at(d) * 2 + yi} for d in range(1, n_z)]
    for peer in peers:
        pl.semaphore_signal(barrier, inc=1, device_id=peer, device_id_type=MESH)
    pl.semaphore_wait(barrier, len(peers))

    pieces = [(g, c) for g in range(groups) for c in range(n_chunks)]
    grad_at = [grad.at[:, pl.ds(g * SUB, SUB), pl.ds(c * chunk, chunk)] for g, c in pieces]

    def x_copy(p, off):
        slot = gathered.at[p, me]
        return remote(grad_at[p], slot, x_send.at[p, off - 1], x_recv.at[p, off - 1], {"exp": chip_at(off) * 2 + core})

    def p_copy(p):
        return remote(grad_at[p], gathered.at[p, me], p_send.at[p], p_recv.at[p], mate)

    def f_copy(p, off):
        slot = gathered.at[p, chip_at(-off) * 2 + core]
        return remote(slot, slot, f_send.at[p, off - 1], f_recv.at[p, off - 1], mate)

    def own_copy(p):
        return pltpu.make_async_copy(grad_at[p], gathered.at[p, me], own_sem.at[p])

    own_half = root_rows.at[core]

    def z_copy(d):
        return remote(own_half, root.at[blk, core], z_send.at[d - 1], z_recv.at[d - 1], {"blk": z_at(d) * 2 + yi})

    def y_copy(d):
        slot = root.at[z_at(-d) * 2 + yi, core]
        return remote(own_half if d == 0 else slot, slot, y_send.at[d], y_recv.at[d], y_peer)

    def c_copy(side, d):
        slot = root.at[z_at(-d) * 2 + (yi if side == 0 else 1 - yi), core]
        return remote(slot, slot, c_send.at[side, d], c_recv.at[side, d], mate)

    root_own = pltpu.make_async_copy(root_rows, root.at[blk], root_sem)

    def mom_copy(g):
        cols = pl.ds(g * SUB, SUB)
        return pltpu.make_async_copy(momentum.at[:, cols, :], out.at[:, cols, :], mom_sem.at[g])

    for off in range(1, chips):
        x_copy(0, off).start()
    y_copy(0).start()
    for d in range(1, n_z):
        z_copy(d).start()
    for p in range(1, len(pieces)):
        for off in range(1, chips):
            x_copy(p, off).start()
    take_mix = pltpu.make_async_copy(expert_hbm, expert_root, mix_sem)
    take_mix.start()
    for p in range(len(pieces)):
        own_copy(p).start()
        p_copy(p).start()
    root_own.start()
    for g in range(groups):
        mom_copy(g).start()

    take_mix.wait()
    experts = expert_root.shape[1]
    spread = lax.broadcasted_iota(jnp.int32, (rows, local_experts), 0) // SUB
    spread = spread == lax.broadcasted_iota(jnp.int32, (rows, local_experts), 1)
    mine = expert_root[pl.ds(pl.multiple_of(me * local_experts, local_experts), local_experts), :]
    tall = jnp.dot(jnp.where(spread, 1.0, 0.0).astype(jnp.bfloat16), mine, preferred_element_type=jnp.float32)
    tall = tall.astype(jnp.bfloat16)

    @pl.loop(0, experts * SUB // TILE)
    def _(t):
        col = t * TILE + lax.broadcasted_iota(jnp.int32, (experts, TILE), 1)
        pick = col // SUB == lax.broadcasted_iota(jnp.int32, (experts, TILE), 0)
        wide = jnp.dot(tall, jnp.where(pick, 1.0, 0.0).astype(jnp.bfloat16), preferred_element_type=jnp.float32)
        same = lax.broadcasted_iota(jnp.int32, (rows, TILE), 0) % SUB == lax.broadcasted_iota(
            jnp.int32, (rows, TILE), 1) % SUB
        mix[:, pl.ds(pl.multiple_of(t * TILE, TILE), TILE)] = jnp.where(same, wide, 0.0).astype(jnp.bfloat16)

    for g in range(groups):
        mom_copy(g).wait()

        @pl.loop(0, local_experts)
        def _(e):
            out[e, pl.ds(g * SUB, SUB)] = 0.9 * out[e, pl.ds(g * SUB, SUB)]

    def blend(p):
        g, c = pieces[p]

        @pl.loop(0, chunk // TILE)
        def _(t):
            lanes = pl.ds(pl.multiple_of(t * TILE, TILE), TILE)
            cols = pl.ds(pl.multiple_of(c * chunk + t * TILE, TILE), TILE)

            def term(k):
                block = gathered[p, pl.ds(k * batch, batch), :, :, lanes].reshape(depth, TILE)
                taps = mix[:, pl.ds(pl.multiple_of(k * depth, depth), depth)]
                return jnp.dot(taps, block, preferred_element_type=jnp.float32)

            acc = term(0)
            if n_exp > batch:
                acc = lax.fori_loop(1, n_exp // batch, lambda k, a: a + term(k), acc)
            blended[g, :, cols] = acc.astype(jnp.bfloat16)

    def apply_root(g, first, last):
        cols = pl.ds(first * chunk, (last - first) * chunk)

        @pl.loop(0, n_blk)
        def _(b):
            taps = root[b, :, :, cols].reshape(slice_rows, (last - first) * chunk)
            part = lax.dot_general(
                blended[g, :, cols], taps, (((1,), (1,)), ((), ())), preferred_element_type=jnp.float32
            )
            dst = pl.ds(pl.multiple_of(b * slice_rows, slice_rows), slice_rows)
            out[:, pl.ds(g * SUB, SUB), dst] += part.reshape(local_experts, SUB, slice_rows)

    def take_z(d):
        z_copy(d).wait_recv()
        y_copy(d).start()
        c_copy(0, d).start()

    def take_y(d):
        y_copy(d).wait_recv()
        c_copy(1, d).start()

    events = [functools.partial(take_z, d) for d in range(1, n_z)]
    events += [functools.partial(take_y, d) for d in range(n_z)]
    ready = len(pieces) * 11 // 16
    done = 0
    pending = 0
    for p, (g, c) in enumerate(pieces):
        for off in range(1, chips):
            x_copy(p, off).wait_recv()
            f_copy(p, off).start()
        goal = len(events) if p >= ready else len(events) * (p + 1) // (ready + 1)
        for event in events[done:goal]:
            event()
        done = goal
        own_copy(p).wait()
        p_copy(p).wait_recv()
        for off in range(1, chips):
            f_copy(p, off).wait_recv()
        blend(p)
        if p == ready:
            root_own.wait()
            for d in range(n_z):
                if d:
                    c_copy(0, d).wait_recv()
                c_copy(1, d).wait_recv()
        if p >= ready and p != len(pieces) - 3:
            while pending <= p and (p > ready or pieces[pending][0] < g):
                gg, first = pieces[pending]
                last = c + 1 if gg == g else n_chunks
                apply_root(gg, first, last)
                pending += last - first

    for p in range(len(pieces)):
        p_copy(p).wait_send()
        for off in range(1, chips):
            x_copy(p, off).wait_send()
            f_copy(p, off).wait_send()
    for d in range(n_z):
        y_copy(d).wait_send()
        c_copy(1, d).wait_send()
        if d:
            z_copy(d).wait_send()
            c_copy(0, d).wait_send()


def expand(expert_root, mix, first_row, row_base, n_rows, first_expert, sub):
    experts, depth = expert_root.shape[1], mix.shape[1]
    rows = n_rows * sub
    spread = lax.broadcasted_iota(jnp.int32, (rows, n_rows), 0) // sub
    spread = spread == lax.broadcasted_iota(jnp.int32, (rows, n_rows), 1)
    taken = expert_root[pl.ds(pl.multiple_of(first_row, n_rows), n_rows), :]
    tall = jnp.dot(jnp.where(spread, 1.0, 0.0).astype(jnp.bfloat16), taken, preferred_element_type=jnp.float32)
    tall = tall.astype(jnp.bfloat16)

    @pl.loop(0, depth // TILE)
    def _(t):
        col = t * TILE + lax.broadcasted_iota(jnp.int32, (experts, TILE), 1)
        pick = first_expert + col // sub == lax.broadcasted_iota(jnp.int32, (experts, TILE), 0)
        wide = jnp.dot(tall, jnp.where(pick, 1.0, 0.0).astype(jnp.bfloat16), preferred_element_type=jnp.float32)
        same = lax.broadcasted_iota(jnp.int32, (rows, TILE), 0) % sub == lax.broadcasted_iota(
            jnp.int32, (rows, TILE), 1) % sub
        lanes = pl.ds(pl.multiple_of(t * TILE, TILE), TILE)
        mix[pl.ds(row_base, rows), lanes] = jnp.where(same, wide, 0.0).astype(jnp.bfloat16)


def remote(src, dst, send, recv, device):
    return pltpu.make_async_remote_copy(
        src_ref=src, dst_ref=dst, send_sem=send, recv_sem=recv, device_id=device, device_id_type=MESH
    )


def gather_kernel(
    n_blk, n_raw,
    *refs,
):
    raws, refs = refs[:n_raw], refs[n_raw:]
    (last, momentum, root_rows, expert_hbm,
     root, base, early, late), refs = refs[:8], refs[8:]
    mates, refs = refs[:n_raw], refs[n_raw:]
    (expert_root, mode, mix, share, z_send, z_recv, own_send, y_send, y_recv, m_send, m_recv,
     mm_send, mm_recv, raw_send, raw_recv, root_sem, mom_sem, mix_sem, out_sem) = refs
    rows, width = last.shape
    local_experts, sub = base.shape[0], base.shape[1]
    half = root.shape[2]
    block = 2 * half
    n_z = n_blk // 2

    me = lax.axis_index("exp")
    chip, core = me // 2, me % 2
    blk = lax.axis_index("blk")
    zi, yi = blk // 2, blk % 2
    mate = {"exp": chip * 2 + 1 - core}
    y_peer = {"blk": zi * 2 + 1 - yi}
    below, above = zi > 0, zi < n_z - 1

    barrier = pltpu.get_barrier_semaphore()
    for peer in (mate, y_peer):
        pl.semaphore_signal(barrier, inc=1, device_id=peer, device_id_type=MESH)

    @pl.when(below)
    def _():
        pl.semaphore_signal(barrier, inc=1, device_id={"blk": blk - 2}, device_id_type=MESH)

    @pl.when(above)
    def _():
        pl.semaphore_signal(barrier, inc=1, device_id={"blk": blk + 2}, device_id_type=MESH)

    pl.semaphore_wait(barrier, jnp.where(below, 1, 0) + jnp.where(above, 1, 0) + 2)

    own_half = root_rows.at[core]

    def nth(t):
        if t == 0:
            return zi
        both = jnp.minimum(zi, n_z - 1 - zi)
        near = zi - (t + 1) // 2 if t % 2 else zi + t // 2
        far = jnp.where(zi < n_z - 1 - zi, zi + (t - both), zi - (t - both))
        return jnp.where(t <= 2 * both, near, far)

    def slot(z, side):
        return root.at[z * 2 + (yi if side == 0 else 1 - yi), core]

    def z_copy(z, step):
        return remote(slot(z, 0), slot(z, 0), z_send.at[z], z_recv.at[z], {"blk": (zi + step) * 2 + yi})

    def own_copy(way, step):
        return remote(own_half, slot(zi, 0), own_send.at[way], z_recv.at[zi], {"blk": (zi + step) * 2 + yi})

    def y_copy(z, t):
        return remote(own_half if t == 0 else slot(z, 0), slot(z, 0), y_send.at[z], y_recv.at[z], y_peer)

    def y_arrival(z):
        return remote(slot(z, 1), slot(z, 1), y_send.at[z], y_recv.at[z], y_peer)

    def m_copy(z, side):
        return remote(slot(z, side), slot(z, side), m_send.at[side, z], m_recv.at[side, z], mate)

    def raw_copy(i):
        return remote(raws[i], mates[i], raw_send.at[i], raw_recv.at[i], mate)

    root_own = pltpu.make_async_copy(root_rows, root.at[blk], root_sem)
    hidden = momentum.shape[1]
    take_mom = pltpu.make_async_copy(momentum.at[:, pl.ds(hidden - sub, sub), :], base, mom_sem)

    def start_own(way, step):
        own_copy(way, step).start()

    pl.when(above)(functools.partial(start_own, 0, 1))
    pl.when(below)(functools.partial(start_own, 1, -1))
    y_copy(zi, 0).start()
    take_mix = pltpu.make_async_copy(expert_hbm, expert_root, mix_sem)
    take_mix.start()
    root_own.start()
    take_mom.start()
    for i in range(n_raw):
        raw_copy(i).start()

    take_mix.wait()
    expand(expert_root, mix, me * local_experts, 0, local_experts, chip * 2 * local_experts, sub)
    expand(expert_root, mix, ((1 - chip) * 2 + core) * local_experts, rows, local_experts, chip * 2 * local_experts, sub)

    def relays(t):
        z = nth(t)
        step = jnp.where(z < zi, 1, -1)
        goes = jnp.where(z < zi, jnp.where(above, 1, 0), jnp.where(below, 1, 0)) == 1
        return z, step, goes

    def take_z(t):
        z, step, goes = relays(t)
        z_copy(z, step).wait_recv()

        @pl.when(goes)
        def _():
            z_copy(z, step).start()

        y_copy(z, t).start()
        m_copy(z, 0).start()

    def take_y(t):
        z = nth(t)
        y_arrival(z).wait_recv()
        m_copy(z, 1).start()

    def lanes_of(b):
        return pl.ds(pl.multiple_of(b * block, block), block)

    def number(t, side):
        return nth(t) * 2 + (yi if side == 0 else 1 - yi)

    def mm_copy(b):
        part = mode.at[b, core]
        return remote(part, part, mm_send.at[b], mm_recv.at[b], mate)

    def model(t, side):
        b = number(t, side)
        if (t, side) == (0, 0):
            root_own.wait()
        else:
            m_copy(nth(t), side).wait_recv()
        part = lax.dot_general(
            last[...], root[b].reshape(block, width), (((1,), (1,)), ((), ())), preferred_element_type=jnp.float32
        )
        mode[b, core] = part.astype(jnp.bfloat16)
        mm_copy(b).start()

    def expert(t, side):
        b = number(t, side)
        mm_copy(b).wait_recv()
        part = jnp.dot(mix[...], mode[b].reshape(2 * rows, block), preferred_element_type=jnp.float32)
        lanes = lanes_of(b)
        base[:, :, lanes] = 0.9 * base[:, :, lanes] + part[:rows].reshape(local_experts, sub, block)
        share[:, lanes] = part[rows:].astype(jnp.bfloat16)

    take_mom.wait()
    model(0, 0)
    events = [(0, 1)]
    for t in range(1, n_z):
        events[-1:-1] = [(t, 0)]
        events.append((t, 1))
    ready = [(0, 0)]
    for i, (t, side) in enumerate(events):
        (take_y if side else take_z)(t)
        if i >= 1:
            model(*events[i - 1])
            expert(*ready.pop(0))
            ready.append(events[i - 1])
    expert(*ready.pop(0))
    model(*events[-1])
    expert(*events[-1])

    cut = early.shape[1]
    outs = [
        pltpu.make_async_copy(share.at[:, pl.ds(0, cut)], early, out_sem.at[0]),
        pltpu.make_async_copy(share.at[:, pl.ds(cut, width - cut)], late, out_sem.at[1]),
    ]
    for copy in outs:
        copy.start()

    pl.when(above)(lambda: own_copy(0, 1).wait_send())
    pl.when(below)(lambda: own_copy(1, -1).wait_send())
    for t in range(n_z):
        z = nth(t)
        if t:
            z, step, goes = relays(t)

            @pl.when(goes)
            def _():
                z_copy(z, step).wait_send()

            m_copy(z, 0).wait_send()
        y_copy(z, t).wait_send()
        m_copy(z, 1).wait_send()
        for side in range(2):
            mm_copy(number(t, side)).wait_send()
    for i in range(n_raw):
        raw_copy(i).wait()
    for copy in outs:
        copy.wait()


def raw_kernel(spans, first, n_after, *refs):
    n_raw = len(spans)
    owns, mates, crosses, refs = refs[:n_raw], refs[n_raw:2 * n_raw], refs[2 * n_raw:3 * n_raw], refs[3 * n_raw + n_after:]
    root, momentum, expert_hbm, out, expert_root, gathered, mix, blended, f_send, f_recv, l_sem, mom_sem, mix_sem = refs
    groups, local_experts, sub, width = out.shape
    rows = local_experts * sub
    n_blk, _, half, _ = root.shape
    block = 2 * half
    n_exp = gathered.shape[1]
    n_cuts = f_send.shape[1]
    cut = width // n_cuts

    me = lax.axis_index("exp")
    chip, core = me // 2, me % 2
    mate_at = chip * 2 + 1 - core
    cross_at = (1 - chip) * 2 + core
    mate = {"exp": mate_at}

    barrier = pltpu.get_barrier_semaphore()
    pl.semaphore_signal(barrier, inc=1, device_id=mate, device_id_type=MESH)
    pl.semaphore_wait(barrier, 1)

    def forward(i, c):
        q, row, count = spans[i]
        lanes = pl.ds(c * cut, cut)
        return remote(
            crosses[i].at[:, lanes], gathered.at[q, cross_at, pl.ds(row, count), lanes], f_send.at[i, c], f_recv.at[i, c], mate
        )

    def arrival(i, c):
        q, row, count = spans[i]
        lanes = pl.ds(c * cut, cut)
        dst = gathered.at[q, (1 - chip) * 2 + 1 - core, pl.ds(row, count), lanes]
        return remote(crosses[i].at[:, lanes], dst, f_send.at[i, c], f_recv.at[i, c], mate)

    def local(i, k):
        q, row, count = spans[i]
        src, at = ((owns[i], me), (mates[i], mate_at), (crosses[i], cross_at))[k]
        return pltpu.make_async_copy(src, gathered.at[q, at, pl.ds(row, count)], l_sem.at[i, k])

    def take_mom(q):
        return pltpu.make_async_copy(momentum.at[:, pl.ds((first + q) * sub, sub), :], out.at[q], mom_sem.at[q])

    for i in range(n_raw):
        for c in range(n_cuts):
            forward(i, c).start()
    take_mix = pltpu.make_async_copy(expert_hbm, expert_root, mix_sem)
    take_mix.start()
    for i in range(n_raw):
        for k in range(3):
            local(i, k).start()
    for q in range(groups):
        take_mom(q).start()

    take_mix.wait()
    expand(expert_root, mix, me * local_experts, 0, local_experts, 0, sub)

    for q in range(groups):
        inside = [i for i in range(n_raw) if spans[i][0] == q]
        for i in inside:
            for k in range(3):
                local(i, k).wait()
        for c in range(n_cuts):
            for i in inside:
                arrival(i, c).wait_recv()
            lanes = pl.ds(c * cut, cut)
            taps = gathered[q, :, :, lanes].reshape(n_exp * rows, cut)
            acc = jnp.dot(mix[...], taps, preferred_element_type=jnp.float32)
            blended[pl.ds(q * rows, rows), lanes] = acc.astype(jnp.bfloat16)
    for q in range(groups):
        take_mom(q).wait()

    @pl.loop(0, n_blk)
    def _(b):
        part = lax.dot_general(
            blended[...], root[b].reshape(block, width), (((1,), (1,)), ((), ())), preferred_element_type=jnp.float32
        )
        lanes = pl.ds(pl.multiple_of(b * block, block), block)
        out[:, :, :, lanes] = 0.9 * out[:, :, :, lanes] + part.reshape(groups, local_experts, sub, block)

    for i in range(n_raw):
        for c in range(n_cuts):
            forward(i, c).wait_send()


def write_kernel(sub, *refs):
    parts, out, sem = refs[:-2], refs[-2], refs[-1]
    copies, first = [], 0
    for part in parts:
        for q in range(part.shape[0]):
            rows = pl.ds((first + q) * sub, sub)
            copies.append(pltpu.make_async_copy(part.at[q], out.at[:, rows, :], sem.at[first + q]))
        first += part.shape[0]
    for copy in copies:
        copy.start()
    for copy in copies:
        copy.wait()


def add_kernel(col, base, share, held, out, total, sem):
    local_experts, sub, width = total.shape
    hidden = out.shape[1]
    lanes = pl.ds(col, width)
    total[...] = base[:, :, lanes] + share[...].reshape(local_experts, sub, width).astype(jnp.float32)
    copy = pltpu.make_async_copy(total, out.at[:, pl.ds(hidden - sub, sub), lanes], sem)
    copy.start()
    copy.wait()


def paired(n_blk, n_exp, grad_block, momentum, model_root, expert_root):
    local_experts, local_hidden, width = grad_block.shape
    experts = expert_root.shape[0]
    sub = local_hidden // 4
    rows = local_experts * sub
    half = model_root.shape[0] // 2
    n_z = n_blk // 2
    lead = local_experts // 4
    cut = width - width // 8
    bf16, f32 = jnp.bfloat16, jnp.float32
    dma = pltpu.SemaphoreType.DMA
    hbm, vmem = pl.BlockSpec(memory_space=pl.ANY), pl.BlockSpec(memory_space=pltpu.VMEM)
    far = pl.BlockSpec(memory_space=pltpu.HBM)
    cost = pl.CostEstimate(flops=2 * 4 * rows * width * width, bytes_accessed=160 << 20, transcendentals=0)
    over_x = [(0, 2), (1, 3), (2, 0), (3, 1)]

    def cross(part):
        return lax.ppermute(part, "exp", over_x)

    def take(array, experts_from, experts_to, q):
        part = array[experts_from:experts_to, q * sub:(q + 1) * sub]
        return part.reshape(-1, width)

    own_0 = take(grad_block, 0, lead, 0)
    cross_0 = cross(own_0)
    rest, own_0 = lax.optimization_barrier((grad_block, own_0))
    own = [own_0, take(rest, lead, local_experts, 0)] + [take(rest, 0, local_experts, q) for q in range(1, 4)]
    raws, last = own[:4], own[4]
    crosses = [cross_0] + [cross(part) for part in raws[1:]]
    spans = [(0, 0, lead * sub), (0, lead * sub, rows - lead * sub), (1, 0, rows), (2, 0, rows)]

    def like(part):
        return jax.ShapeDtypeStruct(part.shape, part.dtype)

    n_raw = len(raws)
    root, base, early, late, *mates = pl.pallas_call(
        functools.partial(gather_kernel, n_blk, n_raw),
        out_shape=[
            pltpu.VMEM((n_blk, 2, half, width), bf16),
            pltpu.VMEM((local_experts, sub, width), f32),
            jax.ShapeDtypeStruct((rows, cut), bf16),
            jax.ShapeDtypeStruct((rows, width - cut), bf16),
        ] + [like(part) for part in raws],
        in_specs=[hbm] * n_raw + [vmem, far, far, far],
        out_specs=[vmem, vmem, hbm, hbm] + [hbm] * n_raw,
        scratch_shapes=[
            pltpu.VMEM(expert_root.shape, bf16),
            pltpu.VMEM((n_blk, 2, rows, 2 * half), bf16),
            pltpu.VMEM((2 * rows, 2 * rows), bf16),
            pltpu.VMEM((rows, width), bf16),
            dma((n_z,)), dma((n_z,)), dma((2,)),
            dma((n_z,)), dma((n_z,)),
            dma((2, n_z)), dma((2, n_z)),
            dma((n_blk,)), dma((n_blk,)),
            dma((n_raw,)), dma((n_raw,)),
            dma, dma, dma, dma((2,)),
        ],
        compiler_params=pltpu.CompilerParams(collective_id=0, has_side_effects=True, vmem_limit_bytes=16 << 20),
        cost_estimate=cost,
    )(*raws, last, momentum, model_root.reshape(2, half, width), expert_root)

    cross_early, cross_late = cross(early), cross(late)

    def blend(first, groups, picked, collective_id, *after):
        inside = [(spans[i][0] - first,) + spans[i][1:] for i in picked]
        n_cuts = 4
        return pl.pallas_call(
            functools.partial(raw_kernel, inside, first, len(after)),
            out_shape=pltpu.VMEM((groups, local_experts, sub, width), f32),
            in_specs=[hbm] * (3 * len(picked) + len(after)) + [vmem, far, far],
            out_specs=vmem,
            scratch_shapes=[
                pltpu.VMEM(expert_root.shape, bf16),
                pltpu.VMEM((groups, n_exp, rows, width), bf16),
                pltpu.VMEM((rows, experts * sub), bf16),
                pltpu.VMEM((groups * rows, width), bf16),
                dma((len(picked), n_cuts)), dma((len(picked), n_cuts)),
                dma((len(picked), 3)), dma((groups,)), dma,
            ],
            compiler_params=pltpu.CompilerParams(
                collective_id=collective_id, has_side_effects=True, vmem_limit_bytes=20 << 20
            ),
            cost_estimate=cost,
        )(
            *[raws[i] for i in picked], *[mates[i] for i in picked], *[crosses[i] for i in picked],
            *after, root, momentum, expert_root,
        )

    upper = blend(0, 2, (0, 1, 2), 1)
    lower = blend(2, 1, (3,), 2, upper)

    whole = jax.ShapeDtypeStruct(momentum.shape, f32)
    out = pl.pallas_call(
        functools.partial(write_kernel, sub),
        out_shape=whole,
        in_specs=[vmem, vmem],
        out_specs=hbm,
        scratch_shapes=[dma((3,))],
        compiler_params=pltpu.CompilerParams(vmem_limit_bytes=8 << 20),
    )(upper, lower)

    def finish(out, share, col):
        return pl.pallas_call(
            functools.partial(add_kernel, col),
            out_shape=whole,
            in_specs=[vmem, vmem, hbm],
            out_specs=hbm,
            scratch_shapes=[pltpu.VMEM((local_experts, sub, share.shape[1]), f32), dma],
            input_output_aliases={2: 0},
            compiler_params=pltpu.CompilerParams(vmem_limit_bytes=8 << 20),
        )(base, share, out)

    return finish(finish(out, cross_early, 0), cross_late, cut)


def solution(mesh):
    n_blk, n_exp = mesh.shape["blk"], mesh.shape["exp"]

    def per_device(grad_block, momentum, model_root, expert_root):
        local_experts, local_hidden, width = grad_block.shape
        if n_exp == 4 and local_hidden % 32 == 0 and local_experts % 8 == 0:
            return paired(n_blk, n_exp, grad_block, momentum, model_root, expert_root)
        experts = expert_root.shape[0]
        groups, n_chunks = local_hidden // SUB, 8
        pieces, rows = groups * n_chunks, local_experts * SUB
        half = model_root.shape[0] // 2
        chips, n_z = n_exp // 2, n_blk // 2
        dma = pltpu.SemaphoreType.DMA
        hbm = pl.BlockSpec(memory_space=pl.ANY)
        return pl.pallas_call(
            functools.partial(kernel, n_blk, n_exp, n_chunks),
            out_shape=pltpu.VMEM(momentum.shape, jnp.float32),
            in_specs=[hbm] * 4,
            out_specs=pl.BlockSpec(memory_space=pltpu.VMEM),
            scratch_shapes=[
                pltpu.VMEM(expert_root.shape, jnp.bfloat16),
                pltpu.VMEM((pieces, n_exp, local_experts, SUB, width // n_chunks), jnp.bfloat16),
                pltpu.VMEM((n_blk, 2, half, width), jnp.bfloat16),
                pltpu.VMEM((rows, experts * SUB), jnp.bfloat16),
                pltpu.VMEM((groups, rows, width), jnp.bfloat16),
                dma((pieces, chips - 1)), dma((pieces, chips - 1)),
                dma((pieces,)), dma((pieces,)),
                dma((pieces, chips - 1)), dma((pieces, chips - 1)),
                dma((pieces,)),
                dma((n_z - 1,)), dma((n_z - 1,)),
                dma((n_z,)), dma((n_z,)),
                dma((2, n_z)), dma((2, n_z)),
                dma, dma((groups,)), dma,
            ],
            compiler_params=pltpu.CompilerParams(
                collective_id=0, has_side_effects=True, vmem_limit_bytes=67_043_328 - 4 * momentum.size
            ),
        )(grad_block, momentum, model_root.reshape(2, half, width), expert_root)

    placed = (P("exp", "blk", None), P("exp", "blk", None), P("blk", None), P())
    return jax.shard_map(
        per_device, mesh=mesh, in_specs=placed, out_specs=P("exp", "blk", None), check_vma=False
    )
```

```python
import functools

import jax
import jax.numpy as jnp
from jax import lax
from jax.experimental import pallas as pl
from jax.experimental.pallas import tpu as pltpu
from jax.sharding import PartitionSpec as P

MESH = pl.DeviceIdType.MESH
SUB = 16
TILE = 256
PARTS = 2


def kernel(
    n_blk, n_exp, n_chunks,
    grad, momentum, root_rows, expert_hbm, out,
    expert_root, gathered, root, mix, blended,
    x_send, x_recv, p_send, p_recv, f_send, f_recv, own_sem,
    z_send, z_recv, y_send, y_recv, c_send, c_recv, root_sem, mom_sem, mix_sem,
):
    local_experts, local_hidden, width = grad.shape
    groups = local_hidden // SUB
    chunk = width // n_chunks
    chips = n_exp // 2
    n_z = n_blk // 2
    rows = local_experts * SUB
    half = root.shape[2]
    batch = 4 if n_exp % 4 == 0 else 2
    depth = batch * rows
    slice_rows = 2 * half

    me = lax.axis_index("exp")
    chip, core = me // 2, me % 2
    blk = lax.axis_index("blk")
    zi, yi = blk // 2, blk % 2
    mate = {"exp": chip * 2 + 1 - core}
    y_peer = {"blk": zi * 2 + 1 - yi}

    def chip_at(offset):
        return lax.rem(chip + offset + chips, chips)

    def z_at(offset):
        return lax.rem(zi + offset + n_z, n_z)

    def remote(src, dst, send, recv, device):
        return pltpu.make_async_remote_copy(
            src_ref=src, dst_ref=dst, send_sem=send, recv_sem=recv, device_id=device, device_id_type=MESH
        )

    barrier = pltpu.get_barrier_semaphore()
    peers = [mate, y_peer]
    peers += [{"exp": chip_at(c) * 2 + core} for c in range(1, chips)]
    peers += [{"blk": z_at(d) * 2 + yi} for d in range(1, n_z)]
    for peer in peers:
        pl.semaphore_signal(barrier, inc=1, device_id=peer, device_id_type=MESH)
    pl.semaphore_wait(barrier, len(peers))

    pieces = [(g, c) for g in range(groups) for c in range(n_chunks)]
    grad_at = [grad.at[:, pl.ds(g * SUB, SUB), pl.ds(c * chunk, chunk)] for g, c in pieces]

    def x_copy(p, off):
        slot = gathered.at[p, me]
        return remote(grad_at[p], slot, x_send.at[p, off - 1], x_recv.at[p, off - 1], {"exp": chip_at(off) * 2 + core})

    def p_copy(p):
        return remote(grad_at[p], gathered.at[p, me], p_send.at[p], p_recv.at[p], mate)

    def f_copy(p, off):
        slot = gathered.at[p, chip_at(-off) * 2 + core]
        return remote(slot, slot, f_send.at[p, off - 1], f_recv.at[p, off - 1], mate)

    def own_copy(p):
        return pltpu.make_async_copy(grad_at[p], gathered.at[p, me], own_sem.at[p])

    own_half = root_rows.at[core]

    def z_copy(d):
        return remote(own_half, root.at[blk, core], z_send.at[d - 1], z_recv.at[d - 1], {"blk": z_at(d) * 2 + yi})

    def y_copy(d):
        slot = root.at[z_at(-d) * 2 + yi, core]
        return remote(own_half if d == 0 else slot, slot, y_send.at[d], y_recv.at[d], y_peer)

    def c_copy(side, d):
        slot = root.at[z_at(-d) * 2 + (yi if side == 0 else 1 - yi), core]
        return remote(slot, slot, c_send.at[side, d], c_recv.at[side, d], mate)

    root_own = pltpu.make_async_copy(root_rows, root.at[blk], root_sem)

    def mom_copy(g):
        cols = pl.ds(g * SUB, SUB)
        return pltpu.make_async_copy(momentum.at[:, cols, :], out.at[:, cols, :], mom_sem.at[g])

    for off in range(1, chips):
        x_copy(0, off).start()
    y_copy(0).start()
    for d in range(1, n_z):
        z_copy(d).start()
    for p in range(1, len(pieces)):
        for off in range(1, chips):
            x_copy(p, off).start()
    take_mix = pltpu.make_async_copy(expert_hbm, expert_root, mix_sem)
    take_mix.start()
    for p in range(len(pieces)):
        own_copy(p).start()
        p_copy(p).start()
    root_own.start()
    for g in range(groups):
        mom_copy(g).start()

    take_mix.wait()
    experts = expert_root.shape[1]
    spread = lax.broadcasted_iota(jnp.int32, (rows, local_experts), 0) // SUB
    spread = spread == lax.broadcasted_iota(jnp.int32, (rows, local_experts), 1)
    mine = expert_root[pl.ds(pl.multiple_of(me * local_experts, local_experts), local_experts), :]
    tall = jnp.dot(jnp.where(spread, 1.0, 0.0).astype(jnp.bfloat16), mine, preferred_element_type=jnp.float32)
    tall = tall.astype(jnp.bfloat16)

    @pl.loop(0, experts * SUB // TILE)
    def _(t):
        col = t * TILE + lax.broadcasted_iota(jnp.int32, (experts, TILE), 1)
        pick = col // SUB == lax.broadcasted_iota(jnp.int32, (experts, TILE), 0)
        wide = jnp.dot(tall, jnp.where(pick, 1.0, 0.0).astype(jnp.bfloat16), preferred_element_type=jnp.float32)
        same = lax.broadcasted_iota(jnp.int32, (rows, TILE), 0) % SUB == lax.broadcasted_iota(
            jnp.int32, (rows, TILE), 1) % SUB
        mix[:, pl.ds(pl.multiple_of(t * TILE, TILE), TILE)] = jnp.where(same, wide, 0.0).astype(jnp.bfloat16)

    for g in range(groups):
        mom_copy(g).wait()

        @pl.loop(0, local_experts)
        def _(e):
            out[e, pl.ds(g * SUB, SUB)] = 0.9 * out[e, pl.ds(g * SUB, SUB)]

    def blend(p):
        g, c = pieces[p]

        @pl.loop(0, chunk // TILE)
        def _(t):
            lanes = pl.ds(pl.multiple_of(t * TILE, TILE), TILE)
            cols = pl.ds(pl.multiple_of(c * chunk + t * TILE, TILE), TILE)

            def term(k):
                block = gathered[p, pl.ds(k * batch, batch), :, :, lanes].reshape(depth, TILE)
                taps = mix[:, pl.ds(pl.multiple_of(k * depth, depth), depth)]
                return jnp.dot(taps, block, preferred_element_type=jnp.float32)

            acc = term(0)
            if n_exp > batch:
                acc = lax.fori_loop(1, n_exp // batch, lambda k, a: a + term(k), acc)
            blended[g, :, cols] = acc.astype(jnp.bfloat16)

    def apply_root(g, first, last):
        cols = pl.ds(first * chunk, (last - first) * chunk)

        @pl.loop(0, n_blk)
        def _(b):
            taps = root[b, :, :, cols].reshape(slice_rows, (last - first) * chunk)
            part = lax.dot_general(
                blended[g, :, cols], taps, (((1,), (1,)), ((), ())), preferred_element_type=jnp.float32
            )
            dst = pl.ds(pl.multiple_of(b * slice_rows, slice_rows), slice_rows)
            out[:, pl.ds(g * SUB, SUB), dst] += part.reshape(local_experts, SUB, slice_rows)

    def take_z(d):
        z_copy(d).wait_recv()
        y_copy(d).start()
        c_copy(0, d).start()

    def take_y(d):
        y_copy(d).wait_recv()
        c_copy(1, d).start()

    events = [functools.partial(take_z, d) for d in range(1, n_z)]
    events += [functools.partial(take_y, d) for d in range(n_z)]
    ready = len(pieces) * 11 // 16
    done = 0
    pending = 0
    for p, (g, c) in enumerate(pieces):
        for off in range(1, chips):
            x_copy(p, off).wait_recv()
            f_copy(p, off).start()
        goal = len(events) if p >= ready else len(events) * (p + 1) // (ready + 1)
        for event in events[done:goal]:
            event()
        done = goal
        own_copy(p).wait()
        p_copy(p).wait_recv()
        for off in range(1, chips):
            f_copy(p, off).wait_recv()
        blend(p)
        if p == ready:
            root_own.wait()
            for d in range(n_z):
                if d:
                    c_copy(0, d).wait_recv()
                c_copy(1, d).wait_recv()
        if p >= ready and p != len(pieces) - 3:
            while pending <= p and (p > ready or pieces[pending][0] < g):
                gg, first = pieces[pending]
                last = c + 1 if gg == g else n_chunks
                apply_root(gg, first, last)
                pending += last - first

    for p in range(len(pieces)):
        p_copy(p).wait_send()
        for off in range(1, chips):
            x_copy(p, off).wait_send()
            f_copy(p, off).wait_send()
    for d in range(n_z):
        y_copy(d).wait_send()
        c_copy(1, d).wait_send()
        if d:
            z_copy(d).wait_send()
            c_copy(0, d).wait_send()


def expand(expert_root, mix, first_row, row_base, n_rows, first_expert, sub, col_base=0, depth=None):
    experts, depth = expert_root.shape[1], depth or mix.shape[1]
    rows = n_rows * sub
    spread = lax.broadcasted_iota(jnp.int32, (rows, n_rows), 0) // sub
    spread = spread == lax.broadcasted_iota(jnp.int32, (rows, n_rows), 1)
    taken = expert_root[pl.ds(pl.multiple_of(first_row, n_rows), n_rows), :]
    tall = jnp.dot(jnp.where(spread, 1.0, 0.0).astype(jnp.bfloat16), taken, preferred_element_type=jnp.float32)
    tall = tall.astype(jnp.bfloat16)

    @pl.loop(0, depth // TILE)
    def _(t):
        col = t * TILE + lax.broadcasted_iota(jnp.int32, (experts, TILE), 1)
        pick = first_expert + col // sub == lax.broadcasted_iota(jnp.int32, (experts, TILE), 0)
        wide = jnp.dot(tall, jnp.where(pick, 1.0, 0.0).astype(jnp.bfloat16), preferred_element_type=jnp.float32)
        same = lax.broadcasted_iota(jnp.int32, (rows, TILE), 0) % sub == lax.broadcasted_iota(
            jnp.int32, (rows, TILE), 1) % sub
        lanes = pl.ds(pl.multiple_of(col_base + t * TILE, TILE), TILE)
        mix[pl.ds(row_base, rows), lanes] = jnp.where(same, wide, 0.0).astype(jnp.bfloat16)


def remote(src, dst, send, recv, device):
    return pltpu.make_async_remote_copy(
        src_ref=src, dst_ref=dst, send_sem=send, recv_sem=recv, device_id=device, device_id_type=MESH
    )


def gather_kernel(
    n_blk, n_raw,
    *refs,
):
    raws, refs = refs[:n_raw], refs[n_raw:]
    (last, root_rows, expert_hbm,
     root, base, early, late, pre, far_mix), refs = refs[:9], refs[9:]
    (expert_root, mates, mode, mix, z_send, z_recv, own_send, y_send, y_recv, m_send, m_recv,
     mm_send, mm_recv, raw_send, raw_recv, root_sem, mix_sem) = refs
    rows, width = last.shape
    local_experts, sub = base.shape[0], base.shape[1]
    half = root.shape[2]
    block = 2 * half
    n_z = n_blk // 2

    me = lax.axis_index("exp")
    chip, core = me // 2, me % 2
    blk = lax.axis_index("blk")
    zi, yi = blk // 2, blk % 2
    mate = {"exp": chip * 2 + 1 - core}
    y_peer = {"blk": zi * 2 + 1 - yi}
    below, above = zi > 0, zi < n_z - 1

    barrier = pltpu.get_barrier_semaphore()
    for peer in (mate, y_peer):
        pl.semaphore_signal(barrier, inc=1, device_id=peer, device_id_type=MESH)

    @pl.when(below)
    def _():
        pl.semaphore_signal(barrier, inc=1, device_id={"blk": blk - 2}, device_id_type=MESH)

    @pl.when(above)
    def _():
        pl.semaphore_signal(barrier, inc=1, device_id={"blk": blk + 2}, device_id_type=MESH)

    pl.semaphore_wait(barrier, jnp.where(below, 1, 0) + jnp.where(above, 1, 0) + 2)

    def nth(t):
        if t == 0:
            return zi
        both = jnp.minimum(zi, n_z - 1 - zi)
        near = zi - (t + 1) // 2 if t % 2 else zi + t // 2
        far = jnp.where(zi < n_z - 1 - zi, zi + (t - both), zi - (t - both))
        return jnp.where(t <= 2 * both, near, far)

    depth = half // PARTS

    def own_part(k):
        return root_rows.at[core, pl.ds(k * depth, depth)]

    def slot(z, side, k):
        return root.at[z * 2 + (yi if side == 0 else 1 - yi), core, pl.ds(k * depth, depth)]

    def z_copy(z, step, k):
        dst = slot(z, 0, k)
        return remote(dst, dst, z_send.at[z, k], z_recv.at[z, k], {"blk": (zi + step) * 2 + yi})

    def own_copy(way, step, k):
        device = {"blk": (zi + step) * 2 + yi}
        return remote(own_part(k), slot(zi, 0, k), own_send.at[way, k], z_recv.at[zi, k], device)

    def y_copy(z, t, k):
        src = slot(z, 0, k) if t else own_part(k)
        return remote(src, slot(z, 0, k), y_send.at[z, k], y_recv.at[z, k], y_peer)

    def y_arrival(z, k):
        dst = slot(z, 1, k)
        return remote(dst, dst, y_send.at[z, k], y_recv.at[z, k], y_peer)

    def m_copy(z, side, k):
        dst = slot(z, side, k)
        return remote(dst, dst, m_send.at[side, z, k], m_recv.at[side, z, k], mate)

    spots = [pl.ds(sum(raw.shape[0] for raw in raws[:i]), raws[i].shape[0]) for i in range(n_raw)]

    def raw_copy(i):
        return remote(raws[i], mates.at[spots[i]], raw_send.at[i], raw_recv.at[i], mate)

    root_own = pltpu.make_async_copy(root_rows, root.at[blk], root_sem)

    def start_own(way, step):
        for k in range(PARTS):
            own_copy(way, step, k).start()

    pl.when(above)(functools.partial(start_own, 0, 1))
    pl.when(below)(functools.partial(start_own, 1, -1))
    for k in range(PARTS):
        y_copy(zi, 0, k).start()
    take_mix = pltpu.make_async_copy(expert_hbm, expert_root, mix_sem)
    take_mix.start()
    root_own.start()
    for i in range(n_raw):
        raw_copy(i).start()

    take_mix.wait()
    expand(expert_root, mix, me * local_experts, 0, local_experts, chip * 2 * local_experts, sub)
    expand(expert_root, mix, ((1 - chip) * 2 + core) * local_experts, rows, local_experts, chip * 2 * local_experts, sub)
    for k in range(2):
        source = (1 - chip) * 2 + (1 - core if k else core)
        expand(expert_root, far_mix, me * local_experts, 0, local_experts, source * local_experts, sub, k * rows, rows)

    def relays(t):
        z = nth(t)
        step = jnp.where(z < zi, 1, -1)
        goes = jnp.where(z < zi, jnp.where(above, 1, 0), jnp.where(below, 1, 0)) == 1
        return z, step, goes

    def take_z(t, k):
        z, step, goes = relays(t)
        z_copy(z, step, k).wait_recv()

        @pl.when(goes)
        def _():
            z_copy(z, step, k).start()

        y_copy(z, t, k).start()
        m_copy(z, 0, k).start()

    def take_y(t, k):
        z = nth(t)
        y_arrival(z, k).wait_recv()
        m_copy(z, 1, k).start()

    def lanes_of(b):
        return pl.ds(pl.multiple_of(b * block, block), block)

    def number(t, side):
        return nth(t) * 2 + (yi if side == 0 else 1 - yi)

    def mm_copy(b):
        part = mode.at[b, core]
        return remote(part, part, mm_send.at[b], mm_recv.at[b], mate)

    def model(t, side):
        b = number(t, side)
        if (t, side) == (0, 0):
            root_own.wait()
        else:
            for k in range(PARTS):
                m_copy(nth(t), side, k).wait_recv()
        part = lax.dot_general(
            last[...], root[b].reshape(block, width), (((1,), (1,)), ((), ())), preferred_element_type=jnp.float32
        )
        mode[b, core] = part.astype(jnp.bfloat16)
        mm_copy(b).start()

    def expert(t, side):
        b = number(t, side)
        mm_copy(b).wait_recv()
        part = jnp.dot(mix[...], mode[b].reshape(2 * rows, block), preferred_element_type=jnp.float32)
        base[:, :, lanes_of(b)] = part[:rows].reshape(local_experts, sub, block)
        share = part[rows:].astype(jnp.bfloat16)

        @pl.when(b < n_blk - 1)
        def _():
            early[:, lanes_of(b)] = share

        @pl.when(b == n_blk - 1)
        def _():
            late[...] = share

    def mix_raw(i):
        own = mix[pl.ds(0, rows), pl.ds(pl.multiple_of(core * rows, rows), rows)]
        other = mix[pl.ds(0, rows), pl.ds(pl.multiple_of((1 - core) * rows, rows), rows)]
        raw_copy(i).wait_recv()

        @pl.loop(0, raws[i].shape[0] // rows)
        def _(q):
            here = pl.ds(pl.multiple_of(q * rows, rows), rows)
            there = pl.ds(pl.multiple_of(spots[i].start + q * rows, rows), rows)
            acc = jnp.dot(own, raws[i][here, :], preferred_element_type=jnp.float32)
            pre[there, :] = acc + jnp.dot(other, mates[there, :], preferred_element_type=jnp.float32)

    model(0, 0)
    events = [(0, 1)]
    for t in range(1, n_z):
        events[-1:-1] = [(t, 0)]
        events.append((t, 1))
    ready = [(0, 0)]
    for i, (t, side) in enumerate(events):
        for k in range(PARTS):
            (take_y if side else take_z)(t, k)
        if i >= 1:
            model(*events[i - 1])
            expert(*ready.pop(0))
            ready.append(events[i - 1])
            if i <= n_raw:
                mix_raw(i - 1)
    expert(*ready.pop(0))
    model(*events[-1])
    expert(*events[-1])

    def end_own(way, step):
        for k in range(PARTS):
            own_copy(way, step, k).wait_send()

    pl.when(above)(functools.partial(end_own, 0, 1))
    pl.when(below)(functools.partial(end_own, 1, -1))
    for t in range(n_z):
        z = nth(t)
        for k in range(PARTS):
            if t:
                z, step, goes = relays(t)

                @pl.when(goes)
                def _():
                    z_copy(z, step, k).wait_send()

                m_copy(z, 0, k).wait_send()
            y_copy(z, t, k).wait_send()
            m_copy(z, 1, k).wait_send()
        for side in range(2):
            mm_copy(number(t, side)).wait_send()
    for i in range(n_raw):
        raw_copy(i).wait_send()


def raw_kernel(n_raw, *refs):
    crosses, refs = refs[:n_raw], refs[n_raw:]
    pre, far_mix, root, momentum, out, fetched, blended, f_send, f_recv, mom_sem = refs
    groups, local_experts, sub, width = out.shape
    rows = local_experts * sub
    n_blk, _, half, _ = root.shape
    block = 2 * half
    n_cuts = f_send.shape[1]
    cut = width // n_cuts

    me = lax.axis_index("exp")
    chip, core = me // 2, me % 2
    mate = {"exp": chip * 2 + 1 - core}

    barrier = pltpu.get_barrier_semaphore()
    pl.semaphore_signal(barrier, inc=1, device_id=mate, device_id_type=MESH)
    pl.semaphore_wait(barrier, 1)

    sources = [(cross, g * rows) for cross in crosses for g in range(cross.shape[0] // rows)]

    def forward(q, c):
        cross, first = sources[q]
        lanes = pl.ds(c * cut, cut)
        dst = fetched.at[pl.ds(q * rows, rows), lanes]
        return remote(cross.at[pl.ds(first, rows), lanes], dst, f_send.at[q, c], f_recv.at[q, c], mate)

    def take_mom(q):
        return pltpu.make_async_copy(momentum.at[:, pl.ds(q * sub, sub), :], out.at[q], mom_sem.at[q])

    for q in range(groups):
        for c in range(n_cuts):
            forward(q, c).start()
    for q in range(groups):
        take_mom(q).start()

    for q in range(groups):
        cross, first = sources[q]
        for c in range(n_cuts):
            lanes = pl.ds(c * cut, cut)
            here = pl.ds(q * rows, rows)
            acc = jnp.dot(far_mix[:, :rows], cross[pl.ds(first, rows), lanes], preferred_element_type=jnp.float32)
            forward(q, c).wait_recv()
            acc += jnp.dot(far_mix[:, rows:], fetched[here, lanes], preferred_element_type=jnp.float32)
            blended[here, lanes] = (pre[here, lanes] + acc).astype(jnp.bfloat16)
    for q in range(groups):
        take_mom(q).wait()

    @pl.loop(0, n_blk)
    def _(b):
        part = lax.dot_general(
            blended[...], root[b].reshape(block, width), (((1,), (1,)), ((), ())), preferred_element_type=jnp.float32
        )
        lanes = pl.ds(pl.multiple_of(b * block, block), block)
        out[:, :, :, lanes] = 0.9 * out[:, :, :, lanes] + part.reshape(groups, local_experts, sub, block)

    for q in range(groups):
        for c in range(n_cuts):
            forward(q, c).wait_send()


def write_kernel(part, base, momentum, out, total, sem):
    groups, _, sub, _ = part.shape
    copies = [pltpu.make_async_copy(part.at[q], out.at[:, pl.ds(q * sub, sub), :], sem.at[q]) for q in range(groups)]
    for copy in copies:
        copy.start()
    take_mom = pltpu.make_async_copy(momentum.at[:, pl.ds(groups * sub, sub), :], total, sem.at[groups])
    take_mom.start()
    take_mom.wait()

    @pl.loop(0, base.shape[0])
    def _(e):
        total[e] = 0.9 * total[e] + base[e]

    for copy in copies:
        copy.wait()


def add_kernel(col, base, share, held, out, total, sem):
    local_experts, sub, width = total.shape
    hidden = out.shape[1]
    lanes = pl.ds(col, width)
    total[...] = base[:, :, lanes] + share[...].reshape(local_experts, sub, width).astype(jnp.float32)
    copy = pltpu.make_async_copy(total, out.at[:, pl.ds(hidden - sub, sub), lanes], sem)
    copy.start()
    copy.wait()


def paired(n_blk, n_exp, grad_block, momentum, model_root, expert_root):
    local_experts, local_hidden, width = grad_block.shape
    sub = local_hidden // 4
    groups = 3
    rows = local_experts * sub
    half = model_root.shape[0] // 2
    n_z = n_blk // 2
    cut = width - 2 * half
    bf16, f32 = jnp.bfloat16, jnp.float32
    dma = pltpu.SemaphoreType.DMA
    hbm, vmem = pl.BlockSpec(memory_space=pl.ANY), pl.BlockSpec(memory_space=pltpu.VMEM)
    cost = pl.CostEstimate(flops=2 * 4 * rows * width * width, bytes_accessed=160 << 20, transcendentals=0)

    def cross(part):
        return lax.ppermute(part, "exp", [(0, 2), (1, 3), (2, 0), (3, 1)])

    def take(array, q):
        return array[:, q * sub:(q + 1) * sub].reshape(rows, width)

    raw_0 = take(grad_block, 0)
    cross_0 = cross(raw_0)
    rest, raw_0 = lax.optimization_barrier((grad_block, raw_0))
    raws = [raw_0] + [take(rest, q) for q in range(1, groups)]
    last = take(rest, groups)
    crosses = [cross_0] + [cross(raw) for raw in raws[1:]]

    n_raw = len(raws)
    root, base, early, late, pre, far_mix = pl.pallas_call(
        functools.partial(gather_kernel, n_blk, n_raw),
        out_shape=[
            pltpu.VMEM((n_blk, 2, half, width), bf16),
            pltpu.VMEM((local_experts, sub, width), f32),
            pltpu.VMEM((rows, cut), bf16),
            pltpu.VMEM((rows, width - cut), bf16),
            pltpu.VMEM((groups * rows, width), f32),
            pltpu.VMEM((rows, 2 * rows), bf16),
        ],
        in_specs=[vmem] * n_raw + [vmem, hbm, hbm],
        out_specs=[vmem] * 6,
        scratch_shapes=[
            pltpu.VMEM(expert_root.shape, bf16),
            pltpu.VMEM((groups * rows, width), bf16),
            pltpu.VMEM((n_blk, 2, rows, 2 * half), bf16),
            pltpu.VMEM((2 * rows, 2 * rows), bf16),
            dma((n_z, PARTS)), dma((n_z, PARTS)), dma((2, PARTS)),
            dma((n_z, PARTS)), dma((n_z, PARTS)),
            dma((2, n_z, PARTS)), dma((2, n_z, PARTS)),
            dma((n_blk,)), dma((n_blk,)),
            dma((n_raw,)), dma((n_raw,)),
            dma, dma,
        ],
        compiler_params=pltpu.CompilerParams(collective_id=0, has_side_effects=True, vmem_limit_bytes=18 << 20),
        cost_estimate=cost,
    )(*raws, last, model_root.reshape(2, half, width), expert_root)

    cross_early, cross_late = cross(early), cross(late)

    n_cuts = 4
    upper = pl.pallas_call(
        functools.partial(raw_kernel, n_raw),
        out_shape=pltpu.VMEM((groups, local_experts, sub, width), f32),
        in_specs=[vmem] * (n_raw + 3) + [hbm],
        out_specs=vmem,
        scratch_shapes=[
            pltpu.VMEM((groups * rows, width), bf16),
            pltpu.VMEM((groups * rows, width), bf16),
            dma((groups, n_cuts)), dma((groups, n_cuts)), dma((groups,)),
        ],
        compiler_params=pltpu.CompilerParams(collective_id=1, has_side_effects=True, vmem_limit_bytes=16 << 20),
        cost_estimate=cost,
    )(*crosses, pre, far_mix, root, momentum)

    whole = jax.ShapeDtypeStruct(momentum.shape, f32)
    out, total = pl.pallas_call(
        write_kernel,
        out_shape=[whole, pltpu.VMEM((local_experts, sub, width), f32)],
        in_specs=[vmem, vmem, hbm],
        out_specs=[hbm, vmem],
        scratch_shapes=[dma((groups + 1,))],
        compiler_params=pltpu.CompilerParams(vmem_limit_bytes=8 << 20),
    )(upper, base, momentum)

    def finish(out, share, col):
        return pl.pallas_call(
            functools.partial(add_kernel, col),
            out_shape=whole,
            in_specs=[vmem, vmem, hbm],
            out_specs=hbm,
            scratch_shapes=[pltpu.VMEM((local_experts, sub, share.shape[1]), f32), dma],
            input_output_aliases={2: 0},
            compiler_params=pltpu.CompilerParams(vmem_limit_bytes=8 << 20),
        )(total, share, out)

    return finish(finish(out, cross_early, 0), cross_late, cut)


def solution(mesh):
    n_blk, n_exp = mesh.shape["blk"], mesh.shape["exp"]

    def per_device(grad_block, momentum, model_root, expert_root):
        local_experts, local_hidden, width = grad_block.shape
        if n_exp == 4 and local_hidden % 32 == 0 and local_experts % 8 == 0:
            return paired(n_blk, n_exp, grad_block, momentum, model_root, expert_root)
        experts = expert_root.shape[0]
        groups, n_chunks = local_hidden // SUB, 8
        pieces, rows = groups * n_chunks, local_experts * SUB
        half = model_root.shape[0] // 2
        chips, n_z = n_exp // 2, n_blk // 2
        dma = pltpu.SemaphoreType.DMA
        hbm = pl.BlockSpec(memory_space=pl.ANY)
        return pl.pallas_call(
            functools.partial(kernel, n_blk, n_exp, n_chunks),
            out_shape=pltpu.VMEM(momentum.shape, jnp.float32),
            in_specs=[hbm] * 4,
            out_specs=pl.BlockSpec(memory_space=pltpu.VMEM),
            scratch_shapes=[
                pltpu.VMEM(expert_root.shape, jnp.bfloat16),
                pltpu.VMEM((pieces, n_exp, local_experts, SUB, width // n_chunks), jnp.bfloat16),
                pltpu.VMEM((n_blk, 2, half, width), jnp.bfloat16),
                pltpu.VMEM((rows, experts * SUB), jnp.bfloat16),
                pltpu.VMEM((groups, rows, width), jnp.bfloat16),
                dma((pieces, chips - 1)), dma((pieces, chips - 1)),
                dma((pieces,)), dma((pieces,)),
                dma((pieces, chips - 1)), dma((pieces, chips - 1)),
                dma((pieces,)),
                dma((n_z - 1,)), dma((n_z - 1,)),
                dma((n_z,)), dma((n_z,)),
                dma((2, n_z)), dma((2, n_z)),
                dma, dma((groups,)), dma,
            ],
            compiler_params=pltpu.CompilerParams(
                collective_id=0, has_side_effects=True, vmem_limit_bytes=67_043_328 - 4 * momentum.size
            ),
        )(grad_block, momentum, model_root.reshape(2, half, width), expert_root)

    placed = (P("exp", "blk", None), P("exp", "blk", None), P("blk", None), P())
    return jax.shard_map(
        per_device, mesh=mesh, in_specs=placed, out_specs=P("exp", "blk", None), check_vma=False
    )
```

```python
import functools

import jax
import jax.numpy as jnp
from jax import lax
from jax.experimental import pallas as pl
from jax.experimental.pallas import tpu as pltpu
from jax.sharding import PartitionSpec as P

MESH = pl.DeviceIdType.MESH
SUB = 16
TILE = 256
PARTS = 2


def kernel(
    n_blk, n_exp, n_chunks,
    grad, momentum, root_rows, expert_hbm, out,
    expert_root, gathered, root, mix, blended,
    x_send, x_recv, p_send, p_recv, f_send, f_recv, own_sem,
    z_send, z_recv, y_send, y_recv, c_send, c_recv, root_sem, mom_sem, mix_sem,
):
    local_experts, local_hidden, width = grad.shape
    groups = local_hidden // SUB
    chunk = width // n_chunks
    chips = n_exp // 2
    n_z = n_blk // 2
    rows = local_experts * SUB
    half = root.shape[2]
    batch = 4 if n_exp % 4 == 0 else 2
    depth = batch * rows
    slice_rows = 2 * half

    me = lax.axis_index("exp")
    chip, core = me // 2, me % 2
    blk = lax.axis_index("blk")
    zi, yi = blk // 2, blk % 2
    mate = {"exp": chip * 2 + 1 - core}
    y_peer = {"blk": zi * 2 + 1 - yi}

    def chip_at(offset):
        return lax.rem(chip + offset + chips, chips)

    def z_at(offset):
        return lax.rem(zi + offset + n_z, n_z)

    def remote(src, dst, send, recv, device):
        return pltpu.make_async_remote_copy(
            src_ref=src, dst_ref=dst, send_sem=send, recv_sem=recv, device_id=device, device_id_type=MESH
        )

    barrier = pltpu.get_barrier_semaphore()
    peers = [mate, y_peer]
    peers += [{"exp": chip_at(c) * 2 + core} for c in range(1, chips)]
    peers += [{"blk": z_at(d) * 2 + yi} for d in range(1, n_z)]
    for peer in peers:
        pl.semaphore_signal(barrier, inc=1, device_id=peer, device_id_type=MESH)
    pl.semaphore_wait(barrier, len(peers))

    pieces = [(g, c) for g in range(groups) for c in range(n_chunks)]
    grad_at = [grad.at[:, pl.ds(g * SUB, SUB), pl.ds(c * chunk, chunk)] for g, c in pieces]

    def x_copy(p, off):
        slot = gathered.at[p, me]
        return remote(grad_at[p], slot, x_send.at[p, off - 1], x_recv.at[p, off - 1], {"exp": chip_at(off) * 2 + core})

    def p_copy(p):
        return remote(grad_at[p], gathered.at[p, me], p_send.at[p], p_recv.at[p], mate)

    def f_copy(p, off):
        slot = gathered.at[p, chip_at(-off) * 2 + core]
        return remote(slot, slot, f_send.at[p, off - 1], f_recv.at[p, off - 1], mate)

    def own_copy(p):
        return pltpu.make_async_copy(grad_at[p], gathered.at[p, me], own_sem.at[p])

    own_half = root_rows.at[core]

    def z_copy(d):
        return remote(own_half, root.at[blk, core], z_send.at[d - 1], z_recv.at[d - 1], {"blk": z_at(d) * 2 + yi})

    def y_copy(d):
        slot = root.at[z_at(-d) * 2 + yi, core]
        return remote(own_half if d == 0 else slot, slot, y_send.at[d], y_recv.at[d], y_peer)

    def c_copy(side, d):
        slot = root.at[z_at(-d) * 2 + (yi if side == 0 else 1 - yi), core]
        return remote(slot, slot, c_send.at[side, d], c_recv.at[side, d], mate)

    root_own = pltpu.make_async_copy(root_rows, root.at[blk], root_sem)

    def mom_copy(g):
        cols = pl.ds(g * SUB, SUB)
        return pltpu.make_async_copy(momentum.at[:, cols, :], out.at[:, cols, :], mom_sem.at[g])

    for off in range(1, chips):
        x_copy(0, off).start()
    y_copy(0).start()
    for d in range(1, n_z):
        z_copy(d).start()
    for p in range(1, len(pieces)):
        for off in range(1, chips):
            x_copy(p, off).start()
    take_mix = pltpu.make_async_copy(expert_hbm, expert_root, mix_sem)
    take_mix.start()
    for p in range(len(pieces)):
        own_copy(p).start()
        p_copy(p).start()
    root_own.start()
    for g in range(groups):
        mom_copy(g).start()

    take_mix.wait()
    experts = expert_root.shape[1]
    spread = lax.broadcasted_iota(jnp.int32, (rows, local_experts), 0) // SUB
    spread = spread == lax.broadcasted_iota(jnp.int32, (rows, local_experts), 1)
    mine = expert_root[pl.ds(pl.multiple_of(me * local_experts, local_experts), local_experts), :]
    tall = jnp.dot(jnp.where(spread, 1.0, 0.0).astype(jnp.bfloat16), mine, preferred_element_type=jnp.float32)
    tall = tall.astype(jnp.bfloat16)

    @pl.loop(0, experts * SUB // TILE)
    def _(t):
        col = t * TILE + lax.broadcasted_iota(jnp.int32, (experts, TILE), 1)
        pick = col // SUB == lax.broadcasted_iota(jnp.int32, (experts, TILE), 0)
        wide = jnp.dot(tall, jnp.where(pick, 1.0, 0.0).astype(jnp.bfloat16), preferred_element_type=jnp.float32)
        same = lax.broadcasted_iota(jnp.int32, (rows, TILE), 0) % SUB == lax.broadcasted_iota(
            jnp.int32, (rows, TILE), 1) % SUB
        mix[:, pl.ds(pl.multiple_of(t * TILE, TILE), TILE)] = jnp.where(same, wide, 0.0).astype(jnp.bfloat16)

    for g in range(groups):
        mom_copy(g).wait()

        @pl.loop(0, local_experts)
        def _(e):
            out[e, pl.ds(g * SUB, SUB)] = 0.9 * out[e, pl.ds(g * SUB, SUB)]

    def blend(p):
        g, c = pieces[p]

        @pl.loop(0, chunk // TILE)
        def _(t):
            lanes = pl.ds(pl.multiple_of(t * TILE, TILE), TILE)
            cols = pl.ds(pl.multiple_of(c * chunk + t * TILE, TILE), TILE)

            def term(k):
                block = gathered[p, pl.ds(k * batch, batch), :, :, lanes].reshape(depth, TILE)
                taps = mix[:, pl.ds(pl.multiple_of(k * depth, depth), depth)]
                return jnp.dot(taps, block, preferred_element_type=jnp.float32)

            acc = term(0)
            if n_exp > batch:
                acc = lax.fori_loop(1, n_exp // batch, lambda k, a: a + term(k), acc)
            blended[g, :, cols] = acc.astype(jnp.bfloat16)

    def apply_root(g, first, last):
        cols = pl.ds(first * chunk, (last - first) * chunk)

        @pl.loop(0, n_blk)
        def _(b):
            taps = root[b, :, :, cols].reshape(slice_rows, (last - first) * chunk)
            part = lax.dot_general(
                blended[g, :, cols], taps, (((1,), (1,)), ((), ())), preferred_element_type=jnp.float32
            )
            dst = pl.ds(pl.multiple_of(b * slice_rows, slice_rows), slice_rows)
            out[:, pl.ds(g * SUB, SUB), dst] += part.reshape(local_experts, SUB, slice_rows)

    def take_z(d):
        z_copy(d).wait_recv()
        y_copy(d).start()
        c_copy(0, d).start()

    def take_y(d):
        y_copy(d).wait_recv()
        c_copy(1, d).start()

    events = [functools.partial(take_z, d) for d in range(1, n_z)]
    events += [functools.partial(take_y, d) for d in range(n_z)]
    ready = len(pieces) * 11 // 16
    done = 0
    pending = 0
    for p, (g, c) in enumerate(pieces):
        for off in range(1, chips):
            x_copy(p, off).wait_recv()
            f_copy(p, off).start()
        goal = len(events) if p >= ready else len(events) * (p + 1) // (ready + 1)
        for event in events[done:goal]:
            event()
        done = goal
        own_copy(p).wait()
        p_copy(p).wait_recv()
        for off in range(1, chips):
            f_copy(p, off).wait_recv()
        blend(p)
        if p == ready:
            root_own.wait()
            for d in range(n_z):
                if d:
                    c_copy(0, d).wait_recv()
                c_copy(1, d).wait_recv()
        if p >= ready and p != len(pieces) - 3:
            while pending <= p and (p > ready or pieces[pending][0] < g):
                gg, first = pieces[pending]
                last = c + 1 if gg == g else n_chunks
                apply_root(gg, first, last)
                pending += last - first

    for p in range(len(pieces)):
        p_copy(p).wait_send()
        for off in range(1, chips):
            x_copy(p, off).wait_send()
            f_copy(p, off).wait_send()
    for d in range(n_z):
        y_copy(d).wait_send()
        c_copy(1, d).wait_send()
        if d:
            z_copy(d).wait_send()
            c_copy(0, d).wait_send()


def expand(expert_root, mix, first_row, row_base, n_rows, first_expert, sub, col_base=0, depth=None):
    experts, depth = expert_root.shape[1], depth or mix.shape[1]
    rows = n_rows * sub
    spread = lax.broadcasted_iota(jnp.int32, (rows, n_rows), 0) // sub
    spread = spread == lax.broadcasted_iota(jnp.int32, (rows, n_rows), 1)
    taken = expert_root[pl.ds(pl.multiple_of(first_row, n_rows), n_rows), :]
    tall = jnp.dot(jnp.where(spread, 1.0, 0.0).astype(jnp.bfloat16), taken, preferred_element_type=jnp.float32)
    tall = tall.astype(jnp.bfloat16)

    @pl.loop(0, depth // TILE)
    def _(t):
        col = t * TILE + lax.broadcasted_iota(jnp.int32, (experts, TILE), 1)
        pick = first_expert + col // sub == lax.broadcasted_iota(jnp.int32, (experts, TILE), 0)
        wide = jnp.dot(tall, jnp.where(pick, 1.0, 0.0).astype(jnp.bfloat16), preferred_element_type=jnp.float32)
        same = lax.broadcasted_iota(jnp.int32, (rows, TILE), 0) % sub == lax.broadcasted_iota(
            jnp.int32, (rows, TILE), 1) % sub
        lanes = pl.ds(pl.multiple_of(col_base + t * TILE, TILE), TILE)
        mix[pl.ds(row_base, rows), lanes] = jnp.where(same, wide, 0.0).astype(jnp.bfloat16)


def remote(src, dst, send, recv, device):
    return pltpu.make_async_remote_copy(
        src_ref=src, dst_ref=dst, send_sem=send, recv_sem=recv, device_id=device, device_id_type=MESH
    )


def gather_kernel(n_blk, spans, *refs):
    n_raw = len(spans)
    raws, refs = refs[:n_raw], refs[n_raw:]
    (last, root_rows, expert_hbm,
     root, base, early, late, pre, far_mix), refs = refs[:9], refs[9:]
    (expert_root, mates, mode, mix, z_send, z_recv, own_send, y_send, y_recv, m_send, m_recv,
     mm_send, mm_recv, raw_send, raw_recv, root_sem, mix_sem) = refs
    rows, width = last.shape
    local_experts, sub = base.shape[0], base.shape[1]
    half = root.shape[2]
    block = 2 * half
    n_z = n_blk // 2

    me = lax.axis_index("exp")
    chip, core = me // 2, me % 2
    blk = lax.axis_index("blk")
    zi, yi = blk // 2, blk % 2
    mate = {"exp": chip * 2 + 1 - core}
    y_peer = {"blk": zi * 2 + 1 - yi}
    below, above = zi > 0, zi < n_z - 1

    barrier = pltpu.get_barrier_semaphore()
    for peer in (mate, y_peer):
        pl.semaphore_signal(barrier, inc=1, device_id=peer, device_id_type=MESH)

    @pl.when(below)
    def _():
        pl.semaphore_signal(barrier, inc=1, device_id={"blk": blk - 2}, device_id_type=MESH)

    @pl.when(above)
    def _():
        pl.semaphore_signal(barrier, inc=1, device_id={"blk": blk + 2}, device_id_type=MESH)

    pl.semaphore_wait(barrier, jnp.where(below, 1, 0) + jnp.where(above, 1, 0) + 2)

    def nth(t):
        if t == 0:
            return zi
        both = jnp.minimum(zi, n_z - 1 - zi)
        near = zi - (t + 1) // 2 if t % 2 else zi + t // 2
        far = jnp.where(zi < n_z - 1 - zi, zi + (t - both), zi - (t - both))
        return jnp.where(t <= 2 * both, near, far)

    depth = half // PARTS

    def own_part(k):
        return root_rows.at[core, pl.ds(k * depth, depth)]

    def slot(z, side, k):
        return root.at[z * 2 + (yi if side == 0 else 1 - yi), core, pl.ds(k * depth, depth)]

    def z_copy(z, step, k):
        dst = slot(z, 0, k)
        return remote(dst, dst, z_send.at[z, k], z_recv.at[z, k], {"blk": (zi + step) * 2 + yi})

    def own_copy(way, step, k):
        device = {"blk": (zi + step) * 2 + yi}
        return remote(own_part(k), slot(zi, 0, k), own_send.at[way, k], z_recv.at[zi, k], device)

    def y_copy(z, t, k):
        src = slot(z, 0, k) if t else own_part(k)
        return remote(src, slot(z, 0, k), y_send.at[z, k], y_recv.at[z, k], y_peer)

    def y_arrival(z, k):
        dst = slot(z, 1, k)
        return remote(dst, dst, y_send.at[z, k], y_recv.at[z, k], y_peer)

    def m_copy(z, side, k):
        dst = slot(z, side, k)
        return remote(dst, dst, m_send.at[side, z, k], m_recv.at[side, z, k], mate)

    def spot(i):
        q, first = spans[i]
        return pl.ds(q * rows, rows), pl.ds(first, raws[i].shape[1])

    def raw_copy(i):
        return remote(raws[i], mates.at[spot(i)], raw_send.at[i], raw_recv.at[i], mate)

    root_own = pltpu.make_async_copy(root_rows, root.at[blk], root_sem)

    def start_own(way, step):
        for k in range(PARTS):
            own_copy(way, step, k).start()

    pl.when(above)(functools.partial(start_own, 0, 1))
    pl.when(below)(functools.partial(start_own, 1, -1))
    for k in range(PARTS):
        y_copy(zi, 0, k).start()
    take_mix = pltpu.make_async_copy(expert_hbm, expert_root, mix_sem)
    take_mix.start()
    root_own.start()
    for i in range(n_raw):
        raw_copy(i).start()

    take_mix.wait()
    expand(expert_root, mix, me * local_experts, 0, local_experts, chip * 2 * local_experts, sub)
    expand(expert_root, mix, ((1 - chip) * 2 + core) * local_experts, rows, local_experts, chip * 2 * local_experts, sub)
    for k in range(2):
        source = (1 - chip) * 2 + (1 - core if k else core)
        expand(expert_root, far_mix, me * local_experts, 0, local_experts, source * local_experts, sub, k * rows, rows)

    def relays(t):
        z = nth(t)
        step = jnp.where(z < zi, 1, -1)
        goes = jnp.where(z < zi, jnp.where(above, 1, 0), jnp.where(below, 1, 0)) == 1
        return z, step, goes

    def take_z(t, k):
        z, step, goes = relays(t)
        z_copy(z, step, k).wait_recv()

        @pl.when(goes)
        def _():
            z_copy(z, step, k).start()

        y_copy(z, t, k).start()
        m_copy(z, 0, k).start()

    def take_y(t, k):
        z = nth(t)
        y_arrival(z, k).wait_recv()
        m_copy(z, 1, k).start()

    def lanes_of(b):
        return pl.ds(pl.multiple_of(b * block, block), block)

    def number(t, side):
        return nth(t) * 2 + (yi if side == 0 else 1 - yi)

    def mm_copy(b):
        part = mode.at[b, core]
        return remote(part, part, mm_send.at[b], mm_recv.at[b], mate)

    def model(t, side):
        b = number(t, side)
        if (t, side) == (0, 0):
            root_own.wait()
        else:
            for k in range(PARTS):
                m_copy(nth(t), side, k).wait_recv()
        part = lax.dot_general(
            last[...], root[b].reshape(block, width), (((1,), (1,)), ((), ())), preferred_element_type=jnp.float32
        )
        mode[b, core] = part.astype(jnp.bfloat16)
        mm_copy(b).start()

    def expert(t, side):
        b = number(t, side)
        mm_copy(b).wait_recv()
        part = jnp.dot(mix[...], mode[b].reshape(2 * rows, block), preferred_element_type=jnp.float32)
        base[:, :, lanes_of(b)] = part[:rows].reshape(local_experts, sub, block)
        share = part[rows:].astype(jnp.bfloat16)

        @pl.when(b < n_blk - 1)
        def _():
            early[:, lanes_of(b)] = share

        @pl.when(b == n_blk - 1)
        def _():
            late[...] = share

    def mix_raw(i):
        own = mix[pl.ds(0, rows), pl.ds(pl.multiple_of(core * rows, rows), rows)]
        other = mix[pl.ds(0, rows), pl.ds(pl.multiple_of((1 - core) * rows, rows), rows)]
        raw_copy(i).wait_recv()
        acc = jnp.dot(own, raws[i][...], preferred_element_type=jnp.float32)
        pre[spot(i)] = acc + jnp.dot(other, mates[spot(i)], preferred_element_type=jnp.float32)

    model(0, 0)
    events = [(0, 1)]
    for t in range(1, n_z):
        events[-1:-1] = [(t, 0)]
        events.append((t, 1))
    ready = [(0, 0)]
    for i, (t, side) in enumerate(events):
        for k in range(PARTS):
            (take_y if side else take_z)(t, k)
        if i >= 1:
            model(*events[i - 1])
            expert(*ready.pop(0))
            ready.append(events[i - 1])
            if i <= n_raw:
                mix_raw(i - 1)
    expert(*ready.pop(0))
    model(*events[-1])
    expert(*events[-1])

    def end_own(way, step):
        for k in range(PARTS):
            own_copy(way, step, k).wait_send()

    pl.when(above)(functools.partial(end_own, 0, 1))
    pl.when(below)(functools.partial(end_own, 1, -1))
    for t in range(n_z):
        z = nth(t)
        for k in range(PARTS):
            if t:
                z, step, goes = relays(t)

                @pl.when(goes)
                def _():
                    z_copy(z, step, k).wait_send()

                m_copy(z, 0, k).wait_send()
            y_copy(z, t, k).wait_send()
            m_copy(z, 1, k).wait_send()
        for side in range(2):
            mm_copy(number(t, side)).wait_send()
    for i in range(n_raw):
        raw_copy(i).wait_send()


def lead_kernel(quarters, lead, sem):
    copy = pltpu.make_async_copy(quarters.at[:, 0, :, pl.ds(0, lead.shape[2])], lead, sem)
    copy.start()
    copy.wait()


def raw_kernel(spans, *refs):
    n_raw = len(spans)
    crosses, refs = refs[:n_raw], refs[n_raw:]
    pre, far_mix, root, momentum, out, fetched, blended, f_send, f_recv, mom_sem = refs
    groups, local_experts, sub, width = out.shape
    rows = local_experts * sub
    n_blk, _, half, _ = root.shape
    block = 2 * half
    n_cuts = f_send.shape[1]
    cut = width // n_cuts

    me = lax.axis_index("exp")
    chip, core = me // 2, me % 2
    mate = {"exp": chip * 2 + 1 - core}

    barrier = pltpu.get_barrier_semaphore()
    pl.semaphore_signal(barrier, inc=1, device_id=mate, device_id_type=MESH)
    pl.semaphore_wait(barrier, 1)

    def piece(q, c):
        i = max(i for i in range(n_raw) if spans[i] <= (q, c * cut))
        return pl.ds(c * cut, cut), crosses[i].at[:, pl.ds(c * cut - spans[i][1], cut)]

    def forward(q, c):
        lanes, src = piece(q, c)
        return remote(src, fetched.at[pl.ds(q * rows, rows), lanes], f_send.at[q, c], f_recv.at[q, c], mate)

    def take_mom(q):
        return pltpu.make_async_copy(momentum.at[:, pl.ds(q * sub, sub), :], out.at[q], mom_sem.at[q])

    for q in range(groups):
        for c in range(n_cuts):
            forward(q, c).start()
    for q in range(groups):
        take_mom(q).start()

    for q in range(groups):
        for c in range(n_cuts):
            lanes, src = piece(q, c)
            here = pl.ds(q * rows, rows)
            acc = jnp.dot(far_mix[:, :rows], src[...], preferred_element_type=jnp.float32)
            forward(q, c).wait_recv()
            acc += jnp.dot(far_mix[:, rows:], fetched[here, lanes], preferred_element_type=jnp.float32)
            blended[here, lanes] = (pre[here, lanes] + acc).astype(jnp.bfloat16)
    for q in range(groups):
        take_mom(q).wait()

    @pl.loop(0, n_blk)
    def _(b):
        part = lax.dot_general(
            blended[...], root[b].reshape(block, width), (((1,), (1,)), ((), ())), preferred_element_type=jnp.float32
        )
        lanes = pl.ds(pl.multiple_of(b * block, block), block)
        out[:, :, :, lanes] = 0.9 * out[:, :, :, lanes] + part.reshape(groups, local_experts, sub, block)

    for q in range(groups):
        for c in range(n_cuts):
            forward(q, c).wait_send()


def write_kernel(part, base, momentum, out, total, sem):
    groups, _, sub, _ = part.shape
    copies = [pltpu.make_async_copy(part.at[q], out.at[:, pl.ds(q * sub, sub), :], sem.at[q]) for q in range(groups)]
    for copy in copies:
        copy.start()
    take_mom = pltpu.make_async_copy(momentum.at[:, pl.ds(groups * sub, sub), :], total, sem.at[groups])
    take_mom.start()
    take_mom.wait()

    @pl.loop(0, base.shape[0])
    def _(e):
        total[e] = 0.9 * total[e] + base[e]

    for copy in copies:
        copy.wait()


def add_kernel(col, base, share, held, out, total, sem):
    local_experts, sub, width = total.shape
    hidden = out.shape[1]
    lanes = pl.ds(col, width)
    total[...] = base[:, :, lanes] + share[...].reshape(local_experts, sub, width).astype(jnp.float32)
    copy = pltpu.make_async_copy(total, out.at[:, pl.ds(hidden - sub, sub), lanes], sem)
    copy.start()
    copy.wait()


def paired(n_blk, n_exp, grad_block, momentum, model_root, expert_root):
    local_experts, local_hidden, width = grad_block.shape
    sub = local_hidden // 4
    groups = 3
    rows = local_experts * sub
    half = model_root.shape[0] // 2
    n_z = n_blk // 2
    cut = width - 2 * half
    bf16, f32 = jnp.bfloat16, jnp.float32
    dma = pltpu.SemaphoreType.DMA
    hbm, vmem = pl.BlockSpec(memory_space=pl.ANY), pl.BlockSpec(memory_space=pltpu.VMEM)
    cost = pl.CostEstimate(flops=2 * 4 * rows * width * width, bytes_accessed=160 << 20, transcendentals=0)

    def cross(part):
        return lax.ppermute(part, "exp", [(0, 2), (1, 3), (2, 0), (3, 1)])

    def take(array, q):
        return array[:, q * sub:(q + 1) * sub].reshape(rows, width)

    n_cuts = 4
    head = width // n_cuts
    lead = pl.pallas_call(
        lead_kernel,
        out_shape=pltpu.VMEM((local_experts, sub, head), bf16),
        in_specs=[hbm],
        out_specs=vmem,
        scratch_shapes=[dma],
        compiler_params=pltpu.CompilerParams(vmem_limit_bytes=60 << 20),
    )(grad_block.reshape(local_experts, 4, sub, width)).reshape(rows, head)
    cross_lead = cross(lead)
    rest, lead = lax.optimization_barrier((grad_block, lead))
    raws = [lead, rest[:, :sub, head:].reshape(rows, width - head)] + [take(rest, q) for q in range(1, groups)]
    last = take(rest, groups)
    crosses = [cross_lead] + [cross(raw) for raw in raws[1:]]
    spans = [(0, 0), (0, head)] + [(q, 0) for q in range(1, groups)]

    n_raw = len(raws)
    root, base, early, late, pre, far_mix = pl.pallas_call(
        functools.partial(gather_kernel, n_blk, spans),
        out_shape=[
            pltpu.VMEM((n_blk, 2, half, width), bf16),
            pltpu.VMEM((local_experts, sub, width), f32),
            pltpu.VMEM((rows, cut), bf16),
            pltpu.VMEM((rows, width - cut), bf16),
            pltpu.VMEM((groups * rows, width), f32),
            pltpu.VMEM((rows, 2 * rows), bf16),
        ],
        in_specs=[vmem] * n_raw + [vmem, hbm, hbm],
        out_specs=[vmem] * 6,
        scratch_shapes=[
            pltpu.VMEM(expert_root.shape, bf16),
            pltpu.VMEM((groups * rows, width), bf16),
            pltpu.VMEM((n_blk, 2, rows, 2 * half), bf16),
            pltpu.VMEM((2 * rows, 2 * rows), bf16),
            dma((n_z, PARTS)), dma((n_z, PARTS)), dma((2, PARTS)),
            dma((n_z, PARTS)), dma((n_z, PARTS)),
            dma((2, n_z, PARTS)), dma((2, n_z, PARTS)),
            dma((n_blk,)), dma((n_blk,)),
            dma((n_raw,)), dma((n_raw,)),
            dma, dma,
        ],
        compiler_params=pltpu.CompilerParams(collective_id=0, has_side_effects=True, vmem_limit_bytes=18 << 20),
        cost_estimate=cost,
    )(*raws, last, model_root.reshape(2, half, width), expert_root)

    cross_early, cross_late = cross(early), cross(late)

    upper = pl.pallas_call(
        functools.partial(raw_kernel, spans),
        out_shape=pltpu.VMEM((groups, local_experts, sub, width), f32),
        in_specs=[vmem] * (n_raw + 3) + [hbm],
        out_specs=vmem,
        scratch_shapes=[
            pltpu.VMEM((groups * rows, width), bf16),
            pltpu.VMEM((groups * rows, width), bf16),
            dma((groups, n_cuts)), dma((groups, n_cuts)), dma((groups,)),
        ],
        compiler_params=pltpu.CompilerParams(collective_id=1, has_side_effects=True, vmem_limit_bytes=16 << 20),
        cost_estimate=cost,
    )(*crosses, pre, far_mix, root, momentum)

    whole = jax.ShapeDtypeStruct(momentum.shape, f32)
    out, total = pl.pallas_call(
        write_kernel,
        out_shape=[whole, pltpu.VMEM((local_experts, sub, width), f32)],
        in_specs=[vmem, vmem, hbm],
        out_specs=[hbm, vmem],
        scratch_shapes=[dma((groups + 1,))],
        compiler_params=pltpu.CompilerParams(vmem_limit_bytes=8 << 20),
    )(upper, base, momentum)

    def finish(out, share, col):
        return pl.pallas_call(
            functools.partial(add_kernel, col),
            out_shape=whole,
            in_specs=[vmem, vmem, hbm],
            out_specs=hbm,
            scratch_shapes=[pltpu.VMEM((local_experts, sub, share.shape[1]), f32), dma],
            input_output_aliases={2: 0},
            compiler_params=pltpu.CompilerParams(vmem_limit_bytes=8 << 20),
        )(total, share, out)

    return finish(finish(out, cross_early, 0), cross_late, cut)


def solution(mesh):
    n_blk, n_exp = mesh.shape["blk"], mesh.shape["exp"]

    def per_device(grad_block, momentum, model_root, expert_root):
        local_experts, local_hidden, width = grad_block.shape
        if n_exp == 4 and local_hidden % 32 == 0 and local_experts % 8 == 0:
            return paired(n_blk, n_exp, grad_block, momentum, model_root, expert_root)
        experts = expert_root.shape[0]
        groups, n_chunks = local_hidden // SUB, 8
        pieces, rows = groups * n_chunks, local_experts * SUB
        half = model_root.shape[0] // 2
        chips, n_z = n_exp // 2, n_blk // 2
        dma = pltpu.SemaphoreType.DMA
        hbm = pl.BlockSpec(memory_space=pl.ANY)
        return pl.pallas_call(
            functools.partial(kernel, n_blk, n_exp, n_chunks),
            out_shape=pltpu.VMEM(momentum.shape, jnp.float32),
            in_specs=[hbm] * 4,
            out_specs=pl.BlockSpec(memory_space=pltpu.VMEM),
            scratch_shapes=[
                pltpu.VMEM(expert_root.shape, jnp.bfloat16),
                pltpu.VMEM((pieces, n_exp, local_experts, SUB, width // n_chunks), jnp.bfloat16),
                pltpu.VMEM((n_blk, 2, half, width), jnp.bfloat16),
                pltpu.VMEM((rows, experts * SUB), jnp.bfloat16),
                pltpu.VMEM((groups, rows, width), jnp.bfloat16),
                dma((pieces, chips - 1)), dma((pieces, chips - 1)),
                dma((pieces,)), dma((pieces,)),
                dma((pieces, chips - 1)), dma((pieces, chips - 1)),
                dma((pieces,)),
                dma((n_z - 1,)), dma((n_z - 1,)),
                dma((n_z,)), dma((n_z,)),
                dma((2, n_z)), dma((2, n_z)),
                dma, dma((groups,)), dma,
            ],
            compiler_params=pltpu.CompilerParams(
                collective_id=0, has_side_effects=True, vmem_limit_bytes=67_043_328 - 4 * momentum.size
            ),
        )(grad_block, momentum, model_root.reshape(2, half, width), expert_root)

    placed = (P("exp", "blk", None), P("exp", "blk", None), P("blk", None), P())
    return jax.shard_map(
        per_device, mesh=mesh, in_specs=placed, out_specs=P("exp", "blk", None), check_vma=False
    )
```

```python
import functools

import jax
import jax.numpy as jnp
from jax import lax
from jax.experimental import pallas as pl
from jax.experimental.pallas import tpu as pltpu
from jax.sharding import PartitionSpec as P

MESH = pl.DeviceIdType.MESH
SUB = 16
TILE = 256
PARTS = 2


def kernel(
    n_blk, n_exp, n_chunks,
    grad, momentum, root_rows, expert_hbm, out,
    expert_root, gathered, root, mix, blended,
    x_send, x_recv, p_send, p_recv, f_send, f_recv, own_sem,
    z_send, z_recv, y_send, y_recv, c_send, c_recv, root_sem, mom_sem, mix_sem,
):
    local_experts, local_hidden, width = grad.shape
    groups = local_hidden // SUB
    chunk = width // n_chunks
    chips = n_exp // 2
    n_z = n_blk // 2
    rows = local_experts * SUB
    half = root.shape[2]
    batch = 4 if n_exp % 4 == 0 else 2
    depth = batch * rows
    slice_rows = 2 * half

    me = lax.axis_index("exp")
    chip, core = me // 2, me % 2
    blk = lax.axis_index("blk")
    zi, yi = blk // 2, blk % 2
    mate = {"exp": chip * 2 + 1 - core}
    y_peer = {"blk": zi * 2 + 1 - yi}

    def chip_at(offset):
        return lax.rem(chip + offset + chips, chips)

    def z_at(offset):
        return lax.rem(zi + offset + n_z, n_z)

    def remote(src, dst, send, recv, device):
        return pltpu.make_async_remote_copy(
            src_ref=src, dst_ref=dst, send_sem=send, recv_sem=recv, device_id=device, device_id_type=MESH
        )

    barrier = pltpu.get_barrier_semaphore()
    peers = [mate, y_peer]
    peers += [{"exp": chip_at(c) * 2 + core} for c in range(1, chips)]
    peers += [{"blk": z_at(d) * 2 + yi} for d in range(1, n_z)]
    for peer in peers:
        pl.semaphore_signal(barrier, inc=1, device_id=peer, device_id_type=MESH)
    pl.semaphore_wait(barrier, len(peers))

    pieces = [(g, c) for g in range(groups) for c in range(n_chunks)]
    grad_at = [grad.at[:, pl.ds(g * SUB, SUB), pl.ds(c * chunk, chunk)] for g, c in pieces]

    def x_copy(p, off):
        slot = gathered.at[p, me]
        return remote(grad_at[p], slot, x_send.at[p, off - 1], x_recv.at[p, off - 1], {"exp": chip_at(off) * 2 + core})

    def p_copy(p):
        return remote(grad_at[p], gathered.at[p, me], p_send.at[p], p_recv.at[p], mate)

    def f_copy(p, off):
        slot = gathered.at[p, chip_at(-off) * 2 + core]
        return remote(slot, slot, f_send.at[p, off - 1], f_recv.at[p, off - 1], mate)

    def own_copy(p):
        return pltpu.make_async_copy(grad_at[p], gathered.at[p, me], own_sem.at[p])

    own_half = root_rows.at[core]

    def z_copy(d):
        return remote(own_half, root.at[blk, core], z_send.at[d - 1], z_recv.at[d - 1], {"blk": z_at(d) * 2 + yi})

    def y_copy(d):
        slot = root.at[z_at(-d) * 2 + yi, core]
        return remote(own_half if d == 0 else slot, slot, y_send.at[d], y_recv.at[d], y_peer)

    def c_copy(side, d):
        slot = root.at[z_at(-d) * 2 + (yi if side == 0 else 1 - yi), core]
        return remote(slot, slot, c_send.at[side, d], c_recv.at[side, d], mate)

    root_own = pltpu.make_async_copy(root_rows, root.at[blk], root_sem)

    def mom_copy(g):
        cols = pl.ds(g * SUB, SUB)
        return pltpu.make_async_copy(momentum.at[:, cols, :], out.at[:, cols, :], mom_sem.at[g])

    for off in range(1, chips):
        x_copy(0, off).start()
    y_copy(0).start()
    for d in range(1, n_z):
        z_copy(d).start()
    for p in range(1, len(pieces)):
        for off in range(1, chips):
            x_copy(p, off).start()
    take_mix = pltpu.make_async_copy(expert_hbm, expert_root, mix_sem)
    take_mix.start()
    for p in range(len(pieces)):
        own_copy(p).start()
        p_copy(p).start()
    root_own.start()
    for g in range(groups):
        mom_copy(g).start()

    take_mix.wait()
    experts = expert_root.shape[1]
    spread = lax.broadcasted_iota(jnp.int32, (rows, local_experts), 0) // SUB
    spread = spread == lax.broadcasted_iota(jnp.int32, (rows, local_experts), 1)
    mine = expert_root[pl.ds(pl.multiple_of(me * local_experts, local_experts), local_experts), :]
    tall = jnp.dot(jnp.where(spread, 1.0, 0.0).astype(jnp.bfloat16), mine, preferred_element_type=jnp.float32)
    tall = tall.astype(jnp.bfloat16)

    @pl.loop(0, experts * SUB // TILE)
    def _(t):
        col = t * TILE + lax.broadcasted_iota(jnp.int32, (experts, TILE), 1)
        pick = col // SUB == lax.broadcasted_iota(jnp.int32, (experts, TILE), 0)
        wide = jnp.dot(tall, jnp.where(pick, 1.0, 0.0).astype(jnp.bfloat16), preferred_element_type=jnp.float32)
        same = lax.broadcasted_iota(jnp.int32, (rows, TILE), 0) % SUB == lax.broadcasted_iota(
            jnp.int32, (rows, TILE), 1) % SUB
        mix[:, pl.ds(pl.multiple_of(t * TILE, TILE), TILE)] = jnp.where(same, wide, 0.0).astype(jnp.bfloat16)

    for g in range(groups):
        mom_copy(g).wait()

        @pl.loop(0, local_experts)
        def _(e):
            out[e, pl.ds(g * SUB, SUB)] = 0.9 * out[e, pl.ds(g * SUB, SUB)]

    def blend(p):
        g, c = pieces[p]

        @pl.loop(0, chunk // TILE)
        def _(t):
            lanes = pl.ds(pl.multiple_of(t * TILE, TILE), TILE)
            cols = pl.ds(pl.multiple_of(c * chunk + t * TILE, TILE), TILE)

            def term(k):
                block = gathered[p, pl.ds(k * batch, batch), :, :, lanes].reshape(depth, TILE)
                taps = mix[:, pl.ds(pl.multiple_of(k * depth, depth), depth)]
                return jnp.dot(taps, block, preferred_element_type=jnp.float32)

            acc = term(0)
            if n_exp > batch:
                acc = lax.fori_loop(1, n_exp // batch, lambda k, a: a + term(k), acc)
            blended[g, :, cols] = acc.astype(jnp.bfloat16)

    def apply_root(g, first, last):
        cols = pl.ds(first * chunk, (last - first) * chunk)

        @pl.loop(0, n_blk)
        def _(b):
            taps = root[b, :, :, cols].reshape(slice_rows, (last - first) * chunk)
            part = lax.dot_general(
                blended[g, :, cols], taps, (((1,), (1,)), ((), ())), preferred_element_type=jnp.float32
            )
            dst = pl.ds(pl.multiple_of(b * slice_rows, slice_rows), slice_rows)
            out[:, pl.ds(g * SUB, SUB), dst] += part.reshape(local_experts, SUB, slice_rows)

    def take_z(d):
        z_copy(d).wait_recv()
        y_copy(d).start()
        c_copy(0, d).start()

    def take_y(d):
        y_copy(d).wait_recv()
        c_copy(1, d).start()

    events = [functools.partial(take_z, d) for d in range(1, n_z)]
    events += [functools.partial(take_y, d) for d in range(n_z)]
    ready = len(pieces) * 11 // 16
    done = 0
    pending = 0
    for p, (g, c) in enumerate(pieces):
        for off in range(1, chips):
            x_copy(p, off).wait_recv()
            f_copy(p, off).start()
        goal = len(events) if p >= ready else len(events) * (p + 1) // (ready + 1)
        for event in events[done:goal]:
            event()
        done = goal
        own_copy(p).wait()
        p_copy(p).wait_recv()
        for off in range(1, chips):
            f_copy(p, off).wait_recv()
        blend(p)
        if p == ready:
            root_own.wait()
            for d in range(n_z):
                if d:
                    c_copy(0, d).wait_recv()
                c_copy(1, d).wait_recv()
        if p >= ready and p != len(pieces) - 3:
            while pending <= p and (p > ready or pieces[pending][0] < g):
                gg, first = pieces[pending]
                last = c + 1 if gg == g else n_chunks
                apply_root(gg, first, last)
                pending += last - first

    for p in range(len(pieces)):
        p_copy(p).wait_send()
        for off in range(1, chips):
            x_copy(p, off).wait_send()
            f_copy(p, off).wait_send()
    for d in range(n_z):
        y_copy(d).wait_send()
        c_copy(1, d).wait_send()
        if d:
            z_copy(d).wait_send()
            c_copy(0, d).wait_send()


def expand(expert_root, mix, first_row, row_base, n_rows, first_expert, sub, col_base=0, depth=None):
    experts, depth = expert_root.shape[1], depth or mix.shape[1]
    rows = n_rows * sub
    spread = lax.broadcasted_iota(jnp.int32, (rows, n_rows), 0) // sub
    spread = spread == lax.broadcasted_iota(jnp.int32, (rows, n_rows), 1)
    taken = expert_root[pl.ds(pl.multiple_of(first_row, n_rows), n_rows), :]
    tall = jnp.dot(jnp.where(spread, 1.0, 0.0).astype(jnp.bfloat16), taken, preferred_element_type=jnp.float32)
    tall = tall.astype(jnp.bfloat16)

    @pl.loop(0, depth // TILE)
    def _(t):
        col = t * TILE + lax.broadcasted_iota(jnp.int32, (experts, TILE), 1)
        pick = first_expert + col // sub == lax.broadcasted_iota(jnp.int32, (experts, TILE), 0)
        wide = jnp.dot(tall, jnp.where(pick, 1.0, 0.0).astype(jnp.bfloat16), preferred_element_type=jnp.float32)
        same = lax.broadcasted_iota(jnp.int32, (rows, TILE), 0) % sub == lax.broadcasted_iota(
            jnp.int32, (rows, TILE), 1) % sub
        lanes = pl.ds(pl.multiple_of(col_base + t * TILE, TILE), TILE)
        mix[pl.ds(row_base, rows), lanes] = jnp.where(same, wide, 0.0).astype(jnp.bfloat16)


def remote(src, dst, send, recv, device):
    return pltpu.make_async_remote_copy(
        src_ref=src, dst_ref=dst, send_sem=send, recv_sem=recv, device_id=device, device_id_type=MESH
    )


def gather_kernel(n_blk, spans, *refs):
    n_raw = len(spans)
    raws, refs = refs[:n_raw], refs[n_raw:]
    (last, root_rows, expert_hbm,
     root, base, early, late, pre, far_mix), refs = refs[:9], refs[9:]
    (expert_root, mates, mode, mix, z_send, z_recv, own_send, y_send, y_recv, m_send, m_recv,
     mm_send, mm_recv, raw_send, raw_recv, root_sem, mix_sem) = refs
    rows, width = last.shape
    local_experts, sub = base.shape[0], base.shape[1]
    half = root.shape[2]
    block = 2 * half
    n_z = n_blk // 2

    me = lax.axis_index("exp")
    chip, core = me // 2, me % 2
    blk = lax.axis_index("blk")
    zi, yi = blk // 2, blk % 2
    mate = {"exp": chip * 2 + 1 - core}
    y_peer = {"blk": zi * 2 + 1 - yi}
    below, above = zi > 0, zi < n_z - 1

    barrier = pltpu.get_barrier_semaphore()
    for peer in (mate, y_peer):
        pl.semaphore_signal(barrier, inc=1, device_id=peer, device_id_type=MESH)

    @pl.when(below)
    def _():
        pl.semaphore_signal(barrier, inc=1, device_id={"blk": blk - 2}, device_id_type=MESH)

    @pl.when(above)
    def _():
        pl.semaphore_signal(barrier, inc=1, device_id={"blk": blk + 2}, device_id_type=MESH)

    pl.semaphore_wait(barrier, jnp.where(below, 1, 0) + jnp.where(above, 1, 0) + 2)

    def nth(t):
        if t == 0:
            return zi
        both = jnp.minimum(zi, n_z - 1 - zi)
        near = zi - (t + 1) // 2 if t % 2 else zi + t // 2
        far = jnp.where(zi < n_z - 1 - zi, zi + (t - both), zi - (t - both))
        return jnp.where(t <= 2 * both, near, far)

    depth = half // PARTS

    def own_part(k):
        return root_rows.at[core, pl.ds(k * depth, depth)]

    def slot(z, side, k):
        return root.at[z * 2 + (yi if side == 0 else 1 - yi), core, pl.ds(k * depth, depth)]

    def z_copy(z, step, k):
        dst = slot(z, 0, k)
        return remote(dst, dst, z_send.at[z, k], z_recv.at[z, k], {"blk": (zi + step) * 2 + yi})

    def z_arrival(z, k):
        dst = slot(z, 0, k)
        return remote(dst, dst, z_send.at[z, k], z_recv.at[z, k], y_peer)

    def own_copy(way, step, k):
        device = {"blk": (zi + step) * 2 + yi}
        return remote(own_part(k), slot(zi, 0, k), own_send.at[way, k], z_recv.at[zi, k], device)

    def y_copy(z, t, k):
        src = slot(z, 0, k) if t else own_part(k)
        return remote(src, slot(z, 0, k), y_send.at[z, k], y_recv.at[z, k], y_peer)

    def y_arrival(z, k):
        dst = slot(z, 1, k)
        return remote(dst, dst, y_send.at[z, k], y_recv.at[z, k], y_peer)

    def m_copy(z, side, k):
        dst = slot(z, side, k)
        return remote(dst, dst, m_send.at[side, z, k], m_recv.at[side, z, k], mate)

    def spot(i):
        q, first = spans[i]
        return pl.ds(q * rows, rows), pl.ds(first, raws[i].shape[1])

    def raw_copy(i):
        return remote(raws[i], mates.at[spot(i)], raw_send.at[i], raw_recv.at[i], mate)

    root_own = pltpu.make_async_copy(root_rows, root.at[blk], root_sem)

    def start_own(way, step):
        for k in range(PARTS):
            own_copy(way, step, k).start()

    pl.when(above)(functools.partial(start_own, 0, 1))
    pl.when(below)(functools.partial(start_own, 1, -1))
    for k in range(PARTS):
        y_copy(zi, 0, k).start()
    take_mix = pltpu.make_async_copy(expert_hbm, expert_root, mix_sem)
    take_mix.start()
    root_own.start()
    for i in range(n_raw):
        raw_copy(i).start()

    take_mix.wait()
    expand(expert_root, mix, me * local_experts, 0, local_experts, chip * 2 * local_experts, sub)
    expand(expert_root, mix, ((1 - chip) * 2 + core) * local_experts, rows, local_experts, chip * 2 * local_experts, sub)
    for k in range(2):
        source = (1 - chip) * 2 + (1 - core if k else core)
        expand(expert_root, far_mix, me * local_experts, 0, local_experts, source * local_experts, sub, k * rows, rows)

    def relays(t):
        z = nth(t)
        step = jnp.where(z < zi, 1, -1)
        goes = jnp.where(z < zi, jnp.where(above, 1, 0), jnp.where(below, 1, 0)) == 1
        return z, step, goes

    def take_z(t, k):
        z, step, goes = relays(t)
        z_arrival(z, k).wait_recv()

        @pl.when(goes)
        def _():
            z_copy(z, step, k).start()

        y_copy(z, t, k).start()
        m_copy(z, 0, k).start()

    def take_y(t, k):
        z = nth(t)
        y_arrival(z, k).wait_recv()
        m_copy(z, 1, k).start()

    def lanes_of(b):
        return pl.ds(pl.multiple_of(b * block, block), block)

    def number(t, side):
        return nth(t) * 2 + (yi if side == 0 else 1 - yi)

    def mm_copy(b):
        part = mode.at[b, core]
        return remote(part, part, mm_send.at[b], mm_recv.at[b], mate)

    def model(t, side):
        b = number(t, side)
        if (t, side) == (0, 0):
            root_own.wait()
        else:
            for k in range(PARTS):
                m_copy(nth(t), side, k).wait_recv()
        part = lax.dot_general(
            last[...], root[b].reshape(block, width), (((1,), (1,)), ((), ())), preferred_element_type=jnp.float32
        )
        mode[b, core] = part.astype(jnp.bfloat16)
        mm_copy(b).start()

    def expert(t, side):
        b = number(t, side)
        mm_copy(b).wait_recv()
        part = jnp.dot(mix[...], mode[b].reshape(2 * rows, block), preferred_element_type=jnp.float32)
        base[:, :, lanes_of(b)] = part[:rows].reshape(local_experts, sub, block)
        share = part[rows:].astype(jnp.bfloat16)

        cut = early.shape[0]
        early[:, lanes_of(b)] = share[:cut]
        late[:, lanes_of(b)] = share[cut:]

    def mix_raw(i):
        own = mix[pl.ds(0, rows), pl.ds(pl.multiple_of(core * rows, rows), rows)]
        other = mix[pl.ds(0, rows), pl.ds(pl.multiple_of((1 - core) * rows, rows), rows)]
        raw_copy(i).wait_recv()
        acc = jnp.dot(own, raws[i][...], preferred_element_type=jnp.float32)
        pre[spot(i)] = acc + jnp.dot(other, mates[spot(i)], preferred_element_type=jnp.float32)

    model(0, 0)
    events = [(0, 1)]
    for t in range(1, n_z):
        events[-1:-1] = [(t, 0)]
        events.append((t, 1))
    ready = [(0, 0)]
    for i, (t, side) in enumerate(events):
        for k in range(PARTS):
            (take_y if side else take_z)(t, k)
        if i >= 1:
            model(*events[i - 1])
            expert(*ready.pop(0))
            ready.append(events[i - 1])
            if i <= n_raw:
                mix_raw(i - 1)
    expert(*ready.pop(0))
    model(*events[-1])
    expert(*events[-1])

    def end_own(way, step):
        for k in range(PARTS):
            own_copy(way, step, k).wait_send()

    pl.when(above)(functools.partial(end_own, 0, 1))
    pl.when(below)(functools.partial(end_own, 1, -1))
    for t in range(n_z):
        z = nth(t)
        for k in range(PARTS):
            if t:
                z, step, goes = relays(t)

                @pl.when(goes)
                def _():
                    z_copy(z, step, k).wait_send()

                m_copy(z, 0, k).wait_send()
            y_copy(z, t, k).wait_send()
            m_copy(z, 1, k).wait_send()
        for side in range(2):
            mm_copy(number(t, side)).wait_send()
    for i in range(n_raw):
        raw_copy(i).wait_send()


def lead_kernel(quarters, lead, sem):
    copy = pltpu.make_async_copy(quarters.at[:, 0, :, pl.ds(0, lead.shape[2])], lead, sem)
    copy.start()
    copy.wait()


def raw_kernel(spans, *refs):
    n_raw = len(spans)
    crosses, refs = refs[:n_raw], refs[n_raw:]
    pre, far_mix, root, momentum, out, fetched, blended, f_send, f_recv, mom_sem = refs
    groups, local_experts, sub, width = out.shape
    rows = local_experts * sub
    n_blk, _, half, _ = root.shape
    block = 2 * half
    n_cuts = f_send.shape[1]
    cut = width // n_cuts

    me = lax.axis_index("exp")
    chip, core = me // 2, me % 2
    mate = {"exp": chip * 2 + 1 - core}

    barrier = pltpu.get_barrier_semaphore()
    pl.semaphore_signal(barrier, inc=1, device_id=mate, device_id_type=MESH)
    pl.semaphore_wait(barrier, 1)

    def piece(q, c):
        i = max(i for i in range(n_raw) if spans[i] <= (q, c * cut))
        return pl.ds(c * cut, cut), crosses[i].at[:, pl.ds(c * cut - spans[i][1], cut)]

    def forward(q, c):
        lanes, src = piece(q, c)
        return remote(src, fetched.at[pl.ds(q * rows, rows), lanes], f_send.at[q, c], f_recv.at[q, c], mate)

    def take_mom(q):
        return pltpu.make_async_copy(momentum.at[:, pl.ds(q * sub, sub), :], out.at[q], mom_sem.at[q])

    for q in range(groups):
        for c in range(n_cuts):
            forward(q, c).start()
    for q in range(groups):
        take_mom(q).start()

    for q in range(groups):
        for c in range(n_cuts):
            lanes, src = piece(q, c)
            here = pl.ds(q * rows, rows)
            acc = jnp.dot(far_mix[:, :rows], src[...], preferred_element_type=jnp.float32)
            forward(q, c).wait_recv()
            acc += jnp.dot(far_mix[:, rows:], fetched[here, lanes], preferred_element_type=jnp.float32)
            blended[here, lanes] = (pre[here, lanes] + acc).astype(jnp.bfloat16)
    for q in range(groups):
        take_mom(q).wait()

    @pl.loop(0, n_blk)
    def _(b):
        part = lax.dot_general(
            blended[...], root[b].reshape(block, width), (((1,), (1,)), ((), ())), preferred_element_type=jnp.float32
        )
        lanes = pl.ds(pl.multiple_of(b * block, block), block)
        out[:, :, :, lanes] = 0.9 * out[:, :, :, lanes] + part.reshape(groups, local_experts, sub, block)

    for q in range(groups):
        for c in range(n_cuts):
            forward(q, c).wait_send()


def write_kernel(part, base, momentum, out, total, sem):
    groups, _, sub, _ = part.shape
    copies = [pltpu.make_async_copy(part.at[q], out.at[:, pl.ds(q * sub, sub), :], sem.at[q]) for q in range(groups)]
    for copy in copies:
        copy.start()
    take_mom = pltpu.make_async_copy(momentum.at[:, pl.ds(groups * sub, sub), :], total, sem.at[groups])
    take_mom.start()
    take_mom.wait()

    @pl.loop(0, base.shape[0])
    def _(e):
        total[e] = 0.9 * total[e] + base[e]

    for copy in copies:
        copy.wait()


def add_kernel(first, base, share, held, out, total, sem):
    count, sub, width = total.shape
    part = pl.ds(first, count)
    total[...] = base[part] + share[...].reshape(count, sub, width).astype(jnp.float32)
    copy = pltpu.make_async_copy(total, out.at[part, pl.ds(out.shape[1] - sub, sub), :], sem)
    copy.start()
    copy.wait()


def paired(n_blk, n_exp, grad_block, momentum, model_root, expert_root):
    local_experts, local_hidden, width = grad_block.shape
    sub = local_hidden // 4
    groups = 3
    rows = local_experts * sub
    half = model_root.shape[0] // 2
    n_z = n_blk // 2
    tail = 4
    cut = (local_experts - tail) * sub
    bf16, f32 = jnp.bfloat16, jnp.float32
    dma = pltpu.SemaphoreType.DMA
    hbm, vmem = pl.BlockSpec(memory_space=pl.ANY), pl.BlockSpec(memory_space=pltpu.VMEM)
    cost = pl.CostEstimate(flops=2 * 4 * rows * width * width, bytes_accessed=160 << 20, transcendentals=0)

    def cross(part):
        return lax.ppermute(part, "exp", [(0, 2), (1, 3), (2, 0), (3, 1)])

    def take(array, q):
        return array[:, q * sub:(q + 1) * sub].reshape(rows, width)

    n_cuts = 4
    head = width // n_cuts
    lead = pl.pallas_call(
        lead_kernel,
        out_shape=pltpu.VMEM((local_experts, sub, head), bf16),
        in_specs=[hbm],
        out_specs=vmem,
        scratch_shapes=[dma],
        compiler_params=pltpu.CompilerParams(vmem_limit_bytes=60 << 20),
    )(grad_block.reshape(local_experts, 4, sub, width)).reshape(rows, head)
    cross_lead = cross(lead)
    rest, lead = lax.optimization_barrier((grad_block, lead))
    raws = [lead, rest[:, :sub, head:].reshape(rows, width - head)] + [take(rest, q) for q in range(1, groups)]
    last = take(rest, groups)
    crosses = [cross_lead] + [cross(raw) for raw in raws[1:]]
    spans = [(0, 0), (0, head)] + [(q, 0) for q in range(1, groups)]

    n_raw = len(raws)
    root, base, early, late, pre, far_mix = pl.pallas_call(
        functools.partial(gather_kernel, n_blk, spans),
        out_shape=[
            pltpu.VMEM((n_blk, 2, half, width), bf16),
            pltpu.VMEM((local_experts, sub, width), f32),
            pltpu.VMEM((cut, width), bf16),
            pltpu.VMEM((rows - cut, width), bf16),
            pltpu.VMEM((groups * rows, width), f32),
            pltpu.VMEM((rows, 2 * rows), bf16),
        ],
        in_specs=[vmem] * n_raw + [vmem, hbm, hbm],
        out_specs=[vmem] * 6,
        scratch_shapes=[
            pltpu.VMEM(expert_root.shape, bf16),
            pltpu.VMEM((groups * rows, width), bf16),
            pltpu.VMEM((n_blk, 2, rows, 2 * half), bf16),
            pltpu.VMEM((2 * rows, 2 * rows), bf16),
            dma((n_z, PARTS)), dma((n_z, PARTS)), dma((2, PARTS)),
            dma((n_z, PARTS)), dma((n_z, PARTS)),
            dma((2, n_z, PARTS)), dma((2, n_z, PARTS)),
            dma((n_blk,)), dma((n_blk,)),
            dma((n_raw,)), dma((n_raw,)),
            dma, dma,
        ],
        compiler_params=pltpu.CompilerParams(collective_id=0, has_side_effects=True, vmem_limit_bytes=18 << 20),
        cost_estimate=cost,
    )(*raws, last, model_root.reshape(2, half, width), expert_root)

    cross_early, cross_late = cross(early), cross(late)

    upper = pl.pallas_call(
        functools.partial(raw_kernel, spans),
        out_shape=pltpu.VMEM((groups, local_experts, sub, width), f32),
        in_specs=[vmem] * (n_raw + 3) + [hbm],
        out_specs=vmem,
        scratch_shapes=[
            pltpu.VMEM((groups * rows, width), bf16),
            pltpu.VMEM((groups * rows, width), bf16),
            dma((groups, n_cuts)), dma((groups, n_cuts)), dma((groups,)),
        ],
        compiler_params=pltpu.CompilerParams(collective_id=1, has_side_effects=True, vmem_limit_bytes=16 << 20),
        cost_estimate=cost,
    )(*crosses, pre, far_mix, root, momentum)

    whole = jax.ShapeDtypeStruct(momentum.shape, f32)
    out, total = pl.pallas_call(
        write_kernel,
        out_shape=[whole, pltpu.VMEM((local_experts, sub, width), f32)],
        in_specs=[vmem, vmem, hbm],
        out_specs=[hbm, vmem],
        scratch_shapes=[dma((groups + 1,))],
        compiler_params=pltpu.CompilerParams(vmem_limit_bytes=8 << 20),
    )(upper, base, momentum)

    def finish(out, share, first):
        return pl.pallas_call(
            functools.partial(add_kernel, first),
            out_shape=whole,
            in_specs=[vmem, vmem, hbm],
            out_specs=hbm,
            scratch_shapes=[pltpu.VMEM((share.shape[0] // sub, sub, width), f32), dma],
            input_output_aliases={2: 0},
            compiler_params=pltpu.CompilerParams(vmem_limit_bytes=8 << 20),
        )(total, share, out)

    return finish(finish(out, cross_early, 0), cross_late, local_experts - tail)


def solution(mesh):
    n_blk, n_exp = mesh.shape["blk"], mesh.shape["exp"]

    def per_device(grad_block, momentum, model_root, expert_root):
        local_experts, local_hidden, width = grad_block.shape
        if n_exp == 4 and local_hidden % 32 == 0 and local_experts * local_hidden % (4 * TILE) == 0:
            return paired(n_blk, n_exp, grad_block, momentum, model_root, expert_root)
        experts = expert_root.shape[0]
        groups, n_chunks = local_hidden // SUB, 8
        pieces, rows = groups * n_chunks, local_experts * SUB
        half = model_root.shape[0] // 2
        chips, n_z = n_exp // 2, n_blk // 2
        dma = pltpu.SemaphoreType.DMA
        hbm = pl.BlockSpec(memory_space=pl.ANY)
        return pl.pallas_call(
            functools.partial(kernel, n_blk, n_exp, n_chunks),
            out_shape=pltpu.VMEM(momentum.shape, jnp.float32),
            in_specs=[hbm] * 4,
            out_specs=pl.BlockSpec(memory_space=pltpu.VMEM),
            scratch_shapes=[
                pltpu.VMEM(expert_root.shape, jnp.bfloat16),
                pltpu.VMEM((pieces, n_exp, local_experts, SUB, width // n_chunks), jnp.bfloat16),
                pltpu.VMEM((n_blk, 2, half, width), jnp.bfloat16),
                pltpu.VMEM((rows, experts * SUB), jnp.bfloat16),
                pltpu.VMEM((groups, rows, width), jnp.bfloat16),
                dma((pieces, chips - 1)), dma((pieces, chips - 1)),
                dma((pieces,)), dma((pieces,)),
                dma((pieces, chips - 1)), dma((pieces, chips - 1)),
                dma((pieces,)),
                dma((n_z - 1,)), dma((n_z - 1,)),
                dma((n_z,)), dma((n_z,)),
                dma((2, n_z)), dma((2, n_z)),
                dma, dma((groups,)), dma,
            ],
            compiler_params=pltpu.CompilerParams(
                collective_id=0, has_side_effects=True, vmem_limit_bytes=67_043_328 - 4 * momentum.size
            ),
        )(grad_block, momentum, model_root.reshape(2, half, width), expert_root)

    placed = (P("exp", "blk", None), P("exp", "blk", None), P("blk", None), P())
    return jax.shard_map(
        per_device, mesh=mesh, in_specs=placed, out_specs=P("exp", "blk", None), check_vma=False
    )
```

```python
import functools

import jax
import jax.numpy as jnp
from jax import lax
from jax.experimental import pallas as pl
from jax.experimental.pallas import tpu as pltpu
from jax.sharding import PartitionSpec as P

MESH = pl.DeviceIdType.MESH
SUB = 16
TILE = 256
PARTS = 2


def kernel(
    n_blk, n_exp, n_chunks,
    grad, momentum, root_rows, expert_hbm, out,
    expert_root, gathered, root, mix, blended,
    x_send, x_recv, p_send, p_recv, f_send, f_recv, own_sem,
    z_send, z_recv, y_send, y_recv, c_send, c_recv, root_sem, mom_sem, mix_sem,
):
    local_experts, local_hidden, width = grad.shape
    groups = local_hidden // SUB
    chunk = width // n_chunks
    chips = n_exp // 2
    n_z = n_blk // 2
    rows = local_experts * SUB
    half = root.shape[2]
    batch = 4 if n_exp % 4 == 0 else 2
    depth = batch * rows
    slice_rows = 2 * half

    me = lax.axis_index("exp")
    chip, core = me // 2, me % 2
    blk = lax.axis_index("blk")
    zi, yi = blk // 2, blk % 2
    mate = {"exp": chip * 2 + 1 - core}
    y_peer = {"blk": zi * 2 + 1 - yi}

    def chip_at(offset):
        return lax.rem(chip + offset + chips, chips)

    def z_at(offset):
        return lax.rem(zi + offset + n_z, n_z)

    def remote(src, dst, send, recv, device):
        return pltpu.make_async_remote_copy(
            src_ref=src, dst_ref=dst, send_sem=send, recv_sem=recv, device_id=device, device_id_type=MESH
        )

    barrier = pltpu.get_barrier_semaphore()
    peers = [mate, y_peer]
    peers += [{"exp": chip_at(c) * 2 + core} for c in range(1, chips)]
    peers += [{"blk": z_at(d) * 2 + yi} for d in range(1, n_z)]
    for peer in peers:
        pl.semaphore_signal(barrier, inc=1, device_id=peer, device_id_type=MESH)
    pl.semaphore_wait(barrier, len(peers))

    pieces = [(g, c) for g in range(groups) for c in range(n_chunks)]
    grad_at = [grad.at[:, pl.ds(g * SUB, SUB), pl.ds(c * chunk, chunk)] for g, c in pieces]

    def x_copy(p, off):
        slot = gathered.at[p, me]
        return remote(grad_at[p], slot, x_send.at[p, off - 1], x_recv.at[p, off - 1], {"exp": chip_at(off) * 2 + core})

    def p_copy(p):
        return remote(grad_at[p], gathered.at[p, me], p_send.at[p], p_recv.at[p], mate)

    def f_copy(p, off):
        slot = gathered.at[p, chip_at(-off) * 2 + core]
        return remote(slot, slot, f_send.at[p, off - 1], f_recv.at[p, off - 1], mate)

    def own_copy(p):
        return pltpu.make_async_copy(grad_at[p], gathered.at[p, me], own_sem.at[p])

    own_half = root_rows.at[core]

    def z_copy(d):
        return remote(own_half, root.at[blk, core], z_send.at[d - 1], z_recv.at[d - 1], {"blk": z_at(d) * 2 + yi})

    def y_copy(d):
        slot = root.at[z_at(-d) * 2 + yi, core]
        return remote(own_half if d == 0 else slot, slot, y_send.at[d], y_recv.at[d], y_peer)

    def c_copy(side, d):
        slot = root.at[z_at(-d) * 2 + (yi if side == 0 else 1 - yi), core]
        return remote(slot, slot, c_send.at[side, d], c_recv.at[side, d], mate)

    root_own = pltpu.make_async_copy(root_rows, root.at[blk], root_sem)

    def mom_copy(g):
        cols = pl.ds(g * SUB, SUB)
        return pltpu.make_async_copy(momentum.at[:, cols, :], out.at[:, cols, :], mom_sem.at[g])

    for off in range(1, chips):
        x_copy(0, off).start()
    y_copy(0).start()
    for d in range(1, n_z):
        z_copy(d).start()
    for p in range(1, len(pieces)):
        for off in range(1, chips):
            x_copy(p, off).start()
    take_mix = pltpu.make_async_copy(expert_hbm, expert_root, mix_sem)
    take_mix.start()
    for p in range(len(pieces)):
        own_copy(p).start()
        p_copy(p).start()
    root_own.start()
    for g in range(groups):
        mom_copy(g).start()

    take_mix.wait()
    experts = expert_root.shape[1]
    spread = lax.broadcasted_iota(jnp.int32, (rows, local_experts), 0) // SUB
    spread = spread == lax.broadcasted_iota(jnp.int32, (rows, local_experts), 1)
    mine = expert_root[pl.ds(pl.multiple_of(me * local_experts, local_experts), local_experts), :]
    tall = jnp.dot(jnp.where(spread, 1.0, 0.0).astype(jnp.bfloat16), mine, preferred_element_type=jnp.float32)
    tall = tall.astype(jnp.bfloat16)

    @pl.loop(0, experts * SUB // TILE)
    def _(t):
        col = t * TILE + lax.broadcasted_iota(jnp.int32, (experts, TILE), 1)
        pick = col // SUB == lax.broadcasted_iota(jnp.int32, (experts, TILE), 0)
        wide = jnp.dot(tall, jnp.where(pick, 1.0, 0.0).astype(jnp.bfloat16), preferred_element_type=jnp.float32)
        same = lax.broadcasted_iota(jnp.int32, (rows, TILE), 0) % SUB == lax.broadcasted_iota(
            jnp.int32, (rows, TILE), 1) % SUB
        mix[:, pl.ds(pl.multiple_of(t * TILE, TILE), TILE)] = jnp.where(same, wide, 0.0).astype(jnp.bfloat16)

    for g in range(groups):
        mom_copy(g).wait()

        @pl.loop(0, local_experts)
        def _(e):
            out[e, pl.ds(g * SUB, SUB)] = 0.9 * out[e, pl.ds(g * SUB, SUB)]

    def blend(p):
        g, c = pieces[p]

        @pl.loop(0, chunk // TILE)
        def _(t):
            lanes = pl.ds(pl.multiple_of(t * TILE, TILE), TILE)
            cols = pl.ds(pl.multiple_of(c * chunk + t * TILE, TILE), TILE)

            def term(k):
                block = gathered[p, pl.ds(k * batch, batch), :, :, lanes].reshape(depth, TILE)
                taps = mix[:, pl.ds(pl.multiple_of(k * depth, depth), depth)]
                return jnp.dot(taps, block, preferred_element_type=jnp.float32)

            acc = term(0)
            if n_exp > batch:
                acc = lax.fori_loop(1, n_exp // batch, lambda k, a: a + term(k), acc)
            blended[g, :, cols] = acc.astype(jnp.bfloat16)

    def apply_root(g, first, last):
        cols = pl.ds(first * chunk, (last - first) * chunk)

        @pl.loop(0, n_blk)
        def _(b):
            taps = root[b, :, :, cols].reshape(slice_rows, (last - first) * chunk)
            part = lax.dot_general(
                blended[g, :, cols], taps, (((1,), (1,)), ((), ())), preferred_element_type=jnp.float32
            )
            dst = pl.ds(pl.multiple_of(b * slice_rows, slice_rows), slice_rows)
            out[:, pl.ds(g * SUB, SUB), dst] += part.reshape(local_experts, SUB, slice_rows)

    def take_z(d):
        z_copy(d).wait_recv()
        y_copy(d).start()
        c_copy(0, d).start()

    def take_y(d):
        y_copy(d).wait_recv()
        c_copy(1, d).start()

    events = [functools.partial(take_z, d) for d in range(1, n_z)]
    events += [functools.partial(take_y, d) for d in range(n_z)]
    ready = len(pieces) * 11 // 16
    done = 0
    pending = 0
    for p, (g, c) in enumerate(pieces):
        for off in range(1, chips):
            x_copy(p, off).wait_recv()
            f_copy(p, off).start()
        goal = len(events) if p >= ready else len(events) * (p + 1) // (ready + 1)
        for event in events[done:goal]:
            event()
        done = goal
        own_copy(p).wait()
        p_copy(p).wait_recv()
        for off in range(1, chips):
            f_copy(p, off).wait_recv()
        blend(p)
        if p == ready:
            root_own.wait()
            for d in range(n_z):
                if d:
                    c_copy(0, d).wait_recv()
                c_copy(1, d).wait_recv()
        if p >= ready and p != len(pieces) - 3:
            while pending <= p and (p > ready or pieces[pending][0] < g):
                gg, first = pieces[pending]
                last = c + 1 if gg == g else n_chunks
                apply_root(gg, first, last)
                pending += last - first

    for p in range(len(pieces)):
        p_copy(p).wait_send()
        for off in range(1, chips):
            x_copy(p, off).wait_send()
            f_copy(p, off).wait_send()
    for d in range(n_z):
        y_copy(d).wait_send()
        c_copy(1, d).wait_send()
        if d:
            z_copy(d).wait_send()
            c_copy(0, d).wait_send()


def expand(expert_root, mix, first_row, row_base, n_rows, first_expert, sub, col_base=0, depth=None):
    experts, depth = expert_root.shape[1], depth or mix.shape[1]
    rows = n_rows * sub
    spread = lax.broadcasted_iota(jnp.int32, (rows, n_rows), 0) // sub
    spread = spread == lax.broadcasted_iota(jnp.int32, (rows, n_rows), 1)
    taken = expert_root[pl.ds(pl.multiple_of(first_row, n_rows), n_rows), :]
    tall = jnp.dot(jnp.where(spread, 1.0, 0.0).astype(jnp.bfloat16), taken, preferred_element_type=jnp.float32)
    tall = tall.astype(jnp.bfloat16)

    @pl.loop(0, depth // TILE)
    def _(t):
        col = t * TILE + lax.broadcasted_iota(jnp.int32, (experts, TILE), 1)
        pick = first_expert + col // sub == lax.broadcasted_iota(jnp.int32, (experts, TILE), 0)
        wide = jnp.dot(tall, jnp.where(pick, 1.0, 0.0).astype(jnp.bfloat16), preferred_element_type=jnp.float32)
        same = lax.broadcasted_iota(jnp.int32, (rows, TILE), 0) % sub == lax.broadcasted_iota(
            jnp.int32, (rows, TILE), 1) % sub
        lanes = pl.ds(pl.multiple_of(col_base + t * TILE, TILE), TILE)
        mix[pl.ds(row_base, rows), lanes] = jnp.where(same, wide, 0.0).astype(jnp.bfloat16)


def remote(src, dst, send, recv, device):
    return pltpu.make_async_remote_copy(
        src_ref=src, dst_ref=dst, send_sem=send, recv_sem=recv, device_id=device, device_id_type=MESH
    )


def gather_kernel(n_blk, spans, *refs):
    n_raw = len(spans)
    raws, refs = refs[:n_raw], refs[n_raw:]
    (last, root_rows, expert_hbm,
     root, base, early, late, pre, far_mix), refs = refs[:9], refs[9:]
    (expert_root, mates, mode, mix, z_send, z_recv, own_send, y_send, y_recv, m_send, m_recv,
     mm_send, mm_recv, raw_send, raw_recv, root_sem, mix_sem) = refs
    rows, width = last.shape
    local_experts, sub = base.shape[0], base.shape[1]
    half = root.shape[2]
    block = 2 * half
    n_z = n_blk // 2

    me = lax.axis_index("exp")
    chip, core = me // 2, me % 2
    blk = lax.axis_index("blk")
    zi, yi = blk // 2, blk % 2
    mate = {"exp": chip * 2 + 1 - core}
    y_peer = {"blk": zi * 2 + 1 - yi}
    below, above = zi > 0, zi < n_z - 1

    barrier = pltpu.get_barrier_semaphore()
    for peer in (mate, y_peer):
        pl.semaphore_signal(barrier, inc=1, device_id=peer, device_id_type=MESH)

    @pl.when(below)
    def _():
        pl.semaphore_signal(barrier, inc=1, device_id={"blk": blk - 2}, device_id_type=MESH)

    @pl.when(above)
    def _():
        pl.semaphore_signal(barrier, inc=1, device_id={"blk": blk + 2}, device_id_type=MESH)

    pl.semaphore_wait(barrier, jnp.where(below, 1, 0) + jnp.where(above, 1, 0) + 2)

    def nth(t):
        if t == 0:
            return zi
        both = jnp.minimum(zi, n_z - 1 - zi)
        near = zi - (t + 1) // 2 if t % 2 else zi + t // 2
        far = jnp.where(zi < n_z - 1 - zi, zi + (t - both), zi - (t - both))
        return jnp.where(t <= 2 * both, near, far)

    depth = half // PARTS

    def own_part(k):
        return root_rows.at[core, pl.ds(k * depth, depth)]

    def slot(z, side, k):
        return root.at[z * 2 + (yi if side == 0 else 1 - yi), core, pl.ds(k * depth, depth)]

    def z_copy(z, step, k):
        dst = slot(z, 0, k)
        return remote(dst, dst, z_send.at[z, k], z_recv.at[z, k], {"blk": (zi + step) * 2 + yi})

    def z_arrival(z, k):
        dst = slot(z, 0, k)
        return remote(dst, dst, z_send.at[z, k], z_recv.at[z, k], y_peer)

    def own_copy(way, step, k):
        device = {"blk": (zi + step) * 2 + yi}
        return remote(own_part(k), slot(zi, 0, k), own_send.at[way, k], z_recv.at[zi, k], device)

    def y_copy(z, t, k):
        src = slot(z, 0, k) if t else own_part(k)
        return remote(src, slot(z, 0, k), y_send.at[z, k], y_recv.at[z, k], y_peer)

    def y_arrival(z, k):
        dst = slot(z, 1, k)
        return remote(dst, dst, y_send.at[z, k], y_recv.at[z, k], y_peer)

    def m_copy(z, side, k):
        dst = slot(z, side, k)
        return remote(dst, dst, m_send.at[side, z, k], m_recv.at[side, z, k], mate)

    def spot(i):
        q, first = spans[i]
        return pl.ds(q * rows, rows), pl.ds(first, raws[i].shape[1])

    def raw_copy(i):
        return remote(raws[i], mates.at[spot(i)], raw_send.at[i], raw_recv.at[i], mate)

    root_own = pltpu.make_async_copy(root_rows, root.at[blk], root_sem)

    def start_own(way, step):
        for k in range(PARTS):
            own_copy(way, step, k).start()

    pl.when(above)(functools.partial(start_own, 0, 1))
    pl.when(below)(functools.partial(start_own, 1, -1))
    for k in range(PARTS):
        y_copy(zi, 0, k).start()
    take_mix = pltpu.make_async_copy(expert_hbm, expert_root, mix_sem)
    take_mix.start()
    root_own.start()
    for i in range(n_raw):
        raw_copy(i).start()

    take_mix.wait()
    expand(expert_root, mix, me * local_experts, 0, local_experts, chip * 2 * local_experts, sub)
    expand(expert_root, mix, ((1 - chip) * 2 + core) * local_experts, rows, local_experts, chip * 2 * local_experts, sub)
    for k in range(2):
        source = (1 - chip) * 2 + (1 - core if k else core)
        expand(expert_root, far_mix, me * local_experts, 0, local_experts, source * local_experts, sub, k * rows, rows)

    def relays(t):
        z = nth(t)
        step = jnp.where(z < zi, 1, -1)
        goes = jnp.where(z < zi, jnp.where(above, 1, 0), jnp.where(below, 1, 0)) == 1
        return z, step, goes

    def take_z(t, k):
        z, step, goes = relays(t)
        z_arrival(z, k).wait_recv()

        @pl.when(goes)
        def _():
            z_copy(z, step, k).start()

        y_copy(z, t, k).start()
        m_copy(z, 0, k).start()

    def take_y(t, k):
        z = nth(t)
        y_arrival(z, k).wait_recv()
        m_copy(z, 1, k).start()

    def lanes_of(b):
        return pl.ds(pl.multiple_of(b * block, block), block)

    def number(t, side):
        return nth(t) * 2 + (yi if side == 0 else 1 - yi)

    def mm_copy(b):
        part = mode.at[b, core]
        return remote(part, part, mm_send.at[b], mm_recv.at[b], mate)

    def model(t, side):
        b = number(t, side)
        if (t, side) == (0, 0):
            root_own.wait()
        else:
            for k in range(PARTS):
                m_copy(nth(t), side, k).wait_recv()
        part = lax.dot_general(
            last[...], root[b].reshape(block, width), (((1,), (1,)), ((), ())), preferred_element_type=jnp.float32
        )
        mode[b, core] = part.astype(jnp.bfloat16)
        mm_copy(b).start()

    def expert(t, side):
        b = number(t, side)
        mm_copy(b).wait_recv()
        part = jnp.dot(mix[...], mode[b].reshape(2 * rows, block), preferred_element_type=jnp.float32)
        base[:, :, lanes_of(b)] = part[:rows].reshape(local_experts, sub, block)
        share = part[rows:].astype(jnp.bfloat16)

        cut = early.shape[0]
        early[:, lanes_of(b)] = share[:cut]
        late[:, lanes_of(b)] = share[cut:]

    def mix_raw(i):
        own = mix[pl.ds(0, rows), pl.ds(pl.multiple_of(core * rows, rows), rows)]
        other = mix[pl.ds(0, rows), pl.ds(pl.multiple_of((1 - core) * rows, rows), rows)]
        raw_copy(i).wait_recv()
        acc = jnp.dot(own, raws[i][...], preferred_element_type=jnp.float32)
        pre[spot(i)] = acc + jnp.dot(other, mates[spot(i)], preferred_element_type=jnp.float32)

    model(0, 0)
    events = [(0, 1)]
    for t in range(1, n_z):
        events[-1:-1] = [(t, 0)]
        events.append((t, 1))
    ready = [(0, 0)]
    for i, (t, side) in enumerate(events):
        for k in range(PARTS):
            (take_y if side else take_z)(t, k)
        if i >= 1:
            model(*events[i - 1])
            expert(*ready.pop(0))
            ready.append(events[i - 1])
            if i <= n_raw:
                mix_raw(i - 1)
    expert(*ready.pop(0))
    model(*events[-1])
    expert(*events[-1])

    def end_own(way, step):
        for k in range(PARTS):
            own_copy(way, step, k).wait_send()

    pl.when(above)(functools.partial(end_own, 0, 1))
    pl.when(below)(functools.partial(end_own, 1, -1))
    for t in range(n_z):
        z = nth(t)
        for k in range(PARTS):
            if t:
                z, step, goes = relays(t)

                @pl.when(goes)
                def _():
                    z_copy(z, step, k).wait_send()

                m_copy(z, 0, k).wait_send()
            y_copy(z, t, k).wait_send()
            m_copy(z, 1, k).wait_send()
        for side in range(2):
            mm_copy(number(t, side)).wait_send()
    for i in range(n_raw):
        raw_copy(i).wait_send()


def lead_kernel(quarters, lead, sem):
    copy = pltpu.make_async_copy(quarters.at[:, 0, :, pl.ds(0, lead.shape[2])], lead, sem)
    copy.start()
    copy.wait()


def raw_kernel(spans, *refs):
    n_raw = len(spans)
    crosses, refs = refs[:n_raw], refs[n_raw:]
    pre, far_mix, root, momentum, out, fetched, blended, f_send, f_recv, mom_sem = refs
    groups, local_experts, sub, width = out.shape
    rows = local_experts * sub
    n_blk, _, half, _ = root.shape
    block = 2 * half
    n_cuts = f_send.shape[1]
    cut = width // n_cuts

    me = lax.axis_index("exp")
    chip, core = me // 2, me % 2
    mate = {"exp": chip * 2 + 1 - core}

    barrier = pltpu.get_barrier_semaphore()
    pl.semaphore_signal(barrier, inc=1, device_id=mate, device_id_type=MESH)
    pl.semaphore_wait(barrier, 1)

    def piece(q, c):
        i = max(i for i in range(n_raw) if spans[i] <= (q, c * cut))
        return pl.ds(c * cut, cut), crosses[i].at[:, pl.ds(c * cut - spans[i][1], cut)]

    def forward(q, c):
        lanes, src = piece(q, c)
        return remote(src, fetched.at[pl.ds(q * rows, rows), lanes], f_send.at[q, c], f_recv.at[q, c], mate)

    def take_mom(q):
        return pltpu.make_async_copy(momentum.at[:, pl.ds(q * sub, sub), :], out.at[q], mom_sem.at[q])

    for q in range(groups):
        for c in range(n_cuts):
            forward(q, c).start()
    for q in range(groups):
        take_mom(q).start()

    for q in range(groups):
        for c in range(n_cuts):
            lanes, src = piece(q, c)
            here = pl.ds(q * rows, rows)
            acc = jnp.dot(far_mix[:, :rows], src[...], preferred_element_type=jnp.float32)
            forward(q, c).wait_recv()
            acc += jnp.dot(far_mix[:, rows:], fetched[here, lanes], preferred_element_type=jnp.float32)
            blended[here, lanes] = (pre[here, lanes] + acc).astype(jnp.bfloat16)
    for q in range(groups):
        take_mom(q).wait()

    @pl.loop(0, n_blk)
    def _(b):
        part = lax.dot_general(
            blended[...], root[b].reshape(block, width), (((1,), (1,)), ((), ())), preferred_element_type=jnp.float32
        )
        lanes = pl.ds(pl.multiple_of(b * block, block), block)
        out[:, :, :, lanes] = 0.9 * out[:, :, :, lanes] + part.reshape(groups, local_experts, sub, block)

    for q in range(groups):
        for c in range(n_cuts):
            forward(q, c).wait_send()


def write_kernel(part, base, momentum, out, total, sem):
    groups, _, sub, _ = part.shape
    copies = [pltpu.make_async_copy(part.at[q], out.at[:, pl.ds(q * sub, sub), :], sem.at[q]) for q in range(groups)]
    for copy in copies:
        copy.start()
    take_mom = pltpu.make_async_copy(momentum.at[:, pl.ds(groups * sub, sub), :], total, sem.at[groups])
    take_mom.start()
    take_mom.wait()

    @pl.loop(0, base.shape[0])
    def _(e):
        total[e] = 0.9 * total[e] + base[e]

    for copy in copies:
        copy.wait()


def pass_kernel(part, *refs):
    out, sem = refs[-2:]
    copy = pltpu.make_async_copy(part, out, sem)
    copy.start()
    copy.wait()


def add_kernel(first, base, *refs):
    shares, (held, out, total, sem) = refs[:-4], refs[-4:]
    count, sub, width = total.shape
    part = pl.ds(first, count)
    core = lax.axis_index("exp") % 2
    for k, share in enumerate(shares):

        @pl.when(core == k if len(shares) > 1 else True)
        def _():
            total[...] = base[part] + share[...].reshape(count, sub, width).astype(jnp.float32)

    copy = pltpu.make_async_copy(total, out.at[part, pl.ds(out.shape[1] - sub, sub), :], sem)
    copy.start()
    copy.wait()


def paired(n_blk, n_exp, grad_block, momentum, model_root, expert_root):
    local_experts, local_hidden, width = grad_block.shape
    sub = local_hidden // 4
    groups = 3
    rows = local_experts * sub
    half = model_root.shape[0] // 2
    n_z = n_blk // 2
    tail = 4
    cut = (local_experts - tail) * sub
    bf16, f32 = jnp.bfloat16, jnp.float32
    dma = pltpu.SemaphoreType.DMA
    hbm, vmem = pl.BlockSpec(memory_space=pl.ANY), pl.BlockSpec(memory_space=pltpu.VMEM)
    cost = pl.CostEstimate(flops=2 * 4 * rows * width * width, bytes_accessed=160 << 20, transcendentals=0)

    def cross(part):
        return lax.ppermute(part, "exp", [(0, 2), (1, 3), (2, 0), (3, 1)])

    def take(array, q):
        return array[:, q * sub:(q + 1) * sub].reshape(rows, width)

    n_cuts = 4
    head = width // n_cuts
    lead = pl.pallas_call(
        lead_kernel,
        out_shape=pltpu.VMEM((local_experts, sub, head), bf16),
        in_specs=[hbm],
        out_specs=vmem,
        scratch_shapes=[dma],
        compiler_params=pltpu.CompilerParams(vmem_limit_bytes=60 << 20),
    )(grad_block.reshape(local_experts, 4, sub, width)).reshape(rows, head)
    cross_lead = cross(lead)
    rest, lead = lax.optimization_barrier((grad_block, lead))
    raws = [lead, rest[:, :sub, head:].reshape(rows, width - head)] + [take(rest, q) for q in range(1, groups)]
    last = take(rest, groups)
    crosses = [cross_lead] + [cross(raw) for raw in raws[1:]]
    spans = [(0, 0), (0, head)] + [(q, 0) for q in range(1, groups)]

    n_raw = len(raws)
    root, base, early, late, pre, far_mix = pl.pallas_call(
        functools.partial(gather_kernel, n_blk, spans),
        out_shape=[
            pltpu.VMEM((n_blk, 2, half, width), bf16),
            pltpu.VMEM((local_experts, sub, width), f32),
            pltpu.VMEM((cut, width), bf16),
            pltpu.VMEM((rows - cut, width), bf16),
            pltpu.VMEM((groups * rows, width), f32),
            pltpu.VMEM((rows, 2 * rows), bf16),
        ],
        in_specs=[vmem] * n_raw + [vmem, hbm, hbm],
        out_specs=[vmem] * 6,
        scratch_shapes=[
            pltpu.VMEM(expert_root.shape, bf16),
            pltpu.VMEM((groups * rows, width), bf16),
            pltpu.VMEM((n_blk, 2, rows, 2 * half), bf16),
            pltpu.VMEM((2 * rows, 2 * rows), bf16),
            dma((n_z, PARTS)), dma((n_z, PARTS)), dma((2, PARTS)),
            dma((n_z, PARTS)), dma((n_z, PARTS)),
            dma((2, n_z, PARTS)), dma((2, n_z, PARTS)),
            dma((n_blk,)), dma((n_blk,)),
            dma((n_raw,)), dma((n_raw,)),
            dma, dma,
        ],
        compiler_params=pltpu.CompilerParams(collective_id=0, has_side_effects=True, vmem_limit_bytes=18 << 20),
        cost_estimate=cost,
    )(*raws, last, model_root.reshape(2, half, width), expert_root)

    def yielded(part):
        return pl.pallas_call(
            pass_kernel,
            out_shape=pltpu.VMEM(part.shape, bf16),
            in_specs=[vmem] + [hbm] * len(crosses),
            out_specs=vmem,
            scratch_shapes=[dma],
            compiler_params=pltpu.CompilerParams(vmem_limit_bytes=8 << 20),
        )(part, *crosses)

    cross_even = lax.ppermute(early, "exp", [(0, 2), (2, 0)])
    cross_odd = lax.ppermute(yielded(early), "exp", [(1, 3), (3, 1)])
    cross_late = cross(late)

    upper = pl.pallas_call(
        functools.partial(raw_kernel, spans),
        out_shape=pltpu.VMEM((groups, local_experts, sub, width), f32),
        in_specs=[vmem] * (n_raw + 3) + [hbm],
        out_specs=vmem,
        scratch_shapes=[
            pltpu.VMEM((groups * rows, width), bf16),
            pltpu.VMEM((groups * rows, width), bf16),
            dma((groups, n_cuts)), dma((groups, n_cuts)), dma((groups,)),
        ],
        compiler_params=pltpu.CompilerParams(collective_id=1, has_side_effects=True, vmem_limit_bytes=16 << 20),
        cost_estimate=cost,
    )(*crosses, pre, far_mix, root, momentum)

    whole = jax.ShapeDtypeStruct(momentum.shape, f32)
    out, total = pl.pallas_call(
        write_kernel,
        out_shape=[whole, pltpu.VMEM((local_experts, sub, width), f32)],
        in_specs=[vmem, vmem, hbm],
        out_specs=[hbm, vmem],
        scratch_shapes=[dma((groups + 1,))],
        compiler_params=pltpu.CompilerParams(vmem_limit_bytes=8 << 20),
    )(upper, base, momentum)

    def finish(out, shares, first):
        size = shares[0].shape[0] // sub
        return pl.pallas_call(
            functools.partial(add_kernel, first),
            out_shape=whole,
            in_specs=[vmem] * (1 + len(shares)) + [hbm],
            out_specs=hbm,
            scratch_shapes=[pltpu.VMEM((size, sub, width), f32), dma],
            input_output_aliases={1 + len(shares): 0},
            compiler_params=pltpu.CompilerParams(vmem_limit_bytes=8 << 20),
        )(total, *shares, out)

    return finish(finish(out, [cross_even, cross_odd], 0), [cross_late], local_experts - tail)


def solution(mesh):
    n_blk, n_exp = mesh.shape["blk"], mesh.shape["exp"]

    def per_device(grad_block, momentum, model_root, expert_root):
        local_experts, local_hidden, width = grad_block.shape
        if n_exp == 4 and local_hidden % 32 == 0 and local_experts * local_hidden % (4 * TILE) == 0:
            return paired(n_blk, n_exp, grad_block, momentum, model_root, expert_root)
        experts = expert_root.shape[0]
        groups, n_chunks = local_hidden // SUB, 8
        pieces, rows = groups * n_chunks, local_experts * SUB
        half = model_root.shape[0] // 2
        chips, n_z = n_exp // 2, n_blk // 2
        dma = pltpu.SemaphoreType.DMA
        hbm = pl.BlockSpec(memory_space=pl.ANY)
        return pl.pallas_call(
            functools.partial(kernel, n_blk, n_exp, n_chunks),
            out_shape=pltpu.VMEM(momentum.shape, jnp.float32),
            in_specs=[hbm] * 4,
            out_specs=pl.BlockSpec(memory_space=pltpu.VMEM),
            scratch_shapes=[
                pltpu.VMEM(expert_root.shape, jnp.bfloat16),
                pltpu.VMEM((pieces, n_exp, local_experts, SUB, width // n_chunks), jnp.bfloat16),
                pltpu.VMEM((n_blk, 2, half, width), jnp.bfloat16),
                pltpu.VMEM((rows, experts * SUB), jnp.bfloat16),
                pltpu.VMEM((groups, rows, width), jnp.bfloat16),
                dma((pieces, chips - 1)), dma((pieces, chips - 1)),
                dma((pieces,)), dma((pieces,)),
                dma((pieces, chips - 1)), dma((pieces, chips - 1)),
                dma((pieces,)),
                dma((n_z - 1,)), dma((n_z - 1,)),
                dma((n_z,)), dma((n_z,)),
                dma((2, n_z)), dma((2, n_z)),
                dma, dma((groups,)), dma,
            ],
            compiler_params=pltpu.CompilerParams(
                collective_id=0, has_side_effects=True, vmem_limit_bytes=67_043_328 - 4 * momentum.size
            ),
        )(grad_block, momentum, model_root.reshape(2, half, width), expert_root)

    placed = (P("exp", "blk", None), P("exp", "blk", None), P("blk", None), P())
    return jax.shard_map(
        per_device, mesh=mesh, in_specs=placed, out_specs=P("exp", "blk", None), check_vma=False
    )
```
